32 devices in a mesh: replica: 2 (over y), fsdp: 4 (over z), tensor: 4 (over x, core).
Axes of the slice: x: 2, y: 2, z: 4, core: 2. Of those that a mesh axis runs over, the one named last changes fastest.
Arguments:
- tokens: bfloat16 [24576, 1024], P(('replica', 'fsdp', 'tensor')), may hold values from -6 to 6
- ln1_gain: float32 [1024], P(('fsdp', 'tensor')), may hold values from 0.5 to 1.5
- ln1_bias: float32 [1024], P(('fsdp', 'tensor')), may hold values from -3 to 3
- qkv_weight: bfloat16 [1024, 3, 1024], P('fsdp', None, 'tensor'), may hold values from -0.1875 to 0.1875
- qv_bias: bfloat16 [2, 16, 64], P(None, 'tensor', 'fsdp'), may hold values from -3 to 3
- out_weight: bfloat16 [1024, 1024], P('tensor', 'fsdp'), may hold values from -0.75 to 0.75
- out_bias: float32 [1024], P(('fsdp', 'tensor')), may hold values from -3 to 3
- ln2_gain: float32 [1024], P(('fsdp', 'tensor')), may hold values from 0.5 to 1.5
- ln2_bias: float32 [1024], P(('fsdp', 'tensor')), may hold values from -3 to 3
- fc_weight: bfloat16 [1024, 4096], P('fsdp', 'tensor'), may hold values from -0.1875 to 0.1875
- fc_bias: bfloat16 [64, 64], P('tensor', 'fsdp'), may hold values from -3 to 3
- proj_weight: bfloat16 [4096, 1024], P('tensor', 'fsdp'), may hold values from -0.09375 to 0.09375
- proj_bias: float32 [1024], P(('fsdp', 'tensor')), may hold values from -3 to 3
- out_grad: bfloat16 [24576, 1024], P(('replica', 'fsdp', 'tensor')), may hold values from -6 to 6
Outputs:
- output: float32 [24576, 1024], P(('replica', 'fsdp', 'tensor'))
- input_grad: float32 [24576, 1024], P(('replica', 'fsdp', 'tensor'))
- grad_ln1_gain: float32 [1024], P(('fsdp', 'tensor'))
- grad_ln1_bias: float32 [1024], P(('fsdp', 'tensor'))
- grad_qkv_weight: float32 [1024, 3, 1024], P('fsdp', None, 'tensor')
- grad_qv_bias: float32 [2, 16, 64], P(None, 'tensor', 'fsdp')
- grad_out_weight: float32 [1024, 1024], P('tensor', 'fsdp')
- grad_out_bias: float32 [1024], P(('fsdp', 'tensor'))
- grad_ln2_gain: float32 [1024], P(('fsdp', 'tensor'))
- grad_ln2_bias: float32 [1024], P(('fsdp', 'tensor'))
- grad_fc_weight: float32 [1024, 4096], P('fsdp', 'tensor')
- grad_fc_bias: float32 [64, 64], P('tensor', 'fsdp')
- grad_proj_weight: float32 [4096, 1024], P('tensor', 'fsdp')
- grad_proj_bias: float32 [1024], P(('fsdp', 'tensor'))
The draws below stay inside these ranges and needn't reach their ends.
All inputs are finite; a program needn't handle non-finite values.
Results may differ from the reference program's by a relative error of at most 0.014.
Values may be sent and summed in bfloat16 or wider, within the bound.
A program may use at most 192 MiB of HBM per device.

```python
import jax
import jax.numpy as jnp
from jax import lax

D = 1024
HEADS = 16
HD = 64
FF = 4096
LEN = 1024
SEQ_GRP = 3
TOK_GRP = 3072
TOKENS = 24576
N_REPLICA = 2
N_FSDP = 4


def steps_of(stream_key, dims, cuts, smallest, high):
    def one(dim, parts):
        draws = jax.random.uniform(jax.random.fold_in(jax.random.fold_in(stream_key, 6), dim), (parts,), jnp.float32, smallest / len(cuts), high / len(cuts))
        return jnp.repeat(jnp.exp(draws), dims[dim] // parts).reshape((-1,) + (1,) * (len(dims) - dim - 1))

    loudness = one(*cuts[0])
    for cut in cuts[1:]:
        loudness = loudness * one(*cut)
    return loudness


def bell_draw(own_key, shape, deviation, reach, cuts=(), held_as=jnp.bfloat16):
    array = deviation * jax.random.normal(own_key, shape, jnp.float32)
    if cuts:
        array = array * steps_of(own_key, shape, cuts, -0.22, 0.18)
    return jnp.clip(array, -reach, reach).astype(held_as)


def setup_inputs(seed: int = 0) -> dict:
    splits = jax.random.split(jax.random.key(seed), 15)
    return {
        "tokens": bell_draw(splits[0], (TOKENS, D), 1.0, 6.0, ((0, 32),)),
        "ln1_gain": jnp.clip(1.0 + 0.1 * jax.random.normal(splits[1], (D,), jnp.float32), 0.5, 1.5),
        "ln1_bias": bell_draw(splits[2], (D,), 0.5, 3.0, ((0, 16),), jnp.float32),
        "qkv_weight": bell_draw(splits[3], (D, 3, D), D ** -0.5, 0.1875, ((0, 4), (2, 4))),
        "qv_bias": bell_draw(splits[4], (2, HEADS, HD), 0.5, 3.0, ((1, 4), (2, 4))),
        "out_weight": bell_draw(splits[5], (D, D), (D // 16) ** -0.5, 0.75, ((0, 4), (1, 4))),
        "out_bias": bell_draw(splits[6], (D,), 0.5, 3.0, ((0, 16),), jnp.float32),
        "ln2_gain": jnp.clip(1.0 + 0.1 * jax.random.normal(splits[7], (D,), jnp.float32), 0.5, 1.5),
        "ln2_bias": bell_draw(splits[8], (D,), 0.5, 3.0, ((0, 16),), jnp.float32),
        "fc_weight": bell_draw(splits[9], (D, FF), D ** -0.5, 0.1875, ((0, 4), (1, 4))),
        "fc_bias": bell_draw(splits[10], (FF // HD, HD), 0.5, 3.0, ((0, 4), (1, 4))),
        "proj_weight": bell_draw(splits[11], (FF, D), FF ** -0.5, 0.09375, ((0, 4), (1, 4))),
        "proj_bias": bell_draw(splits[12], (D,), 0.5, 3.0, ((0, 16),), jnp.float32),
        "out_grad": bell_draw(splits[13], (TOKENS, D), 1.0, 6.0, ((0, 32),)),
    }


EPS = 1e-05
NEG = -1e+30

@jax.custom_vjp
def low(v):
    return lax.optimization_barrier(v.astype(jnp.bfloat16)).astype(jnp.float32)

@jax.custom_vjp
def low_back(v):
    return v

def low_keep(v):
    return (low(v), None)

def low_pass(kept, grad):
    return (grad,)

def back_keep(v):
    return (v, None)

def back_low(kept, grad):
    return (low(grad),)
low.defvjp(low_keep, low_pass)
low_back.defvjp(back_keep, back_low)

def layer_norm(values, gain, bias):
    center = values - lax.optimization_barrier(jnp.mean(values, -1, keepdims=True))
    spread = lax.optimization_barrier(jnp.mean(center * center, -1, keepdims=True))
    return center * lax.rsqrt(spread + EPS) * gain + bias

def product(left, right):
    return jnp.dot(left, right, precision=lax.Precision.HIGHEST)

def attend_sequence(item):
    query, keys, values = item
    scores = jnp.einsum('qhd,khd->hqk', query, keys, precision=lax.Precision.HIGHEST) * HD ** (-0.5)
    scores = low_back(scores)
    allowed = jnp.arange(LEN)[:, None] >= jnp.arange(LEN)[None, :]
    scores = jnp.where(allowed[None], scores, NEG)
    weights = low(jax.nn.softmax(scores, axis=-1))
    return jnp.einsum('hqk,khd->qhd', weights, values, precision=lax.Precision.HIGHEST)

def group_forward(params, inputs):
    gain_one, bias_one, qkv_w, qv_b, out_w, out_b, gain_two, bias_two, fc_w, fc_b, proj_w, proj_b = params
    normed_one = low(layer_norm(inputs, gain_one, bias_one))
    query = low_back(low(product(normed_one, qkv_w[:, 0, :]) + qv_b[0].reshape(D)))
    keys = low_back(low(product(normed_one, qkv_w[:, 1, :])))
    values = low_back(low(product(normed_one, qkv_w[:, 2, :]) + qv_b[1].reshape(D)))
    grid_shape = (SEQ_GRP, LEN, HEADS, HD)
    attended = lax.map(jax.checkpoint(attend_sequence), (query.reshape(grid_shape), keys.reshape(grid_shape), values.reshape(grid_shape)))
    attended = low_back(low(attended.reshape(TOK_GRP, D)))
    branch = low_back(product(attended, out_w) + out_b)
    middle = inputs + branch
    normed_two = low(layer_norm(middle, gain_two, bias_two))
    before = low_back(product(normed_two, fc_w) + fc_b.reshape(FF))
    activated = low(jax.nn.gelu(before, approximate=True))
    return middle + product(activated, proj_w) + proj_b

def reference(tokens, ln1_gain, ln1_bias, qkv_weight, qv_bias, out_weight, out_bias, ln2_gain, ln2_bias, fc_weight, fc_bias, proj_weight, proj_bias, out_grad):
    params = tuple((arr.astype(jnp.float32) for arr in (ln1_gain, ln1_bias, qkv_weight, qv_bias, out_weight, out_bias, ln2_gain, ln2_bias, fc_weight, fc_bias, proj_weight, proj_bias)))
    groups = N_REPLICA * N_FSDP
    inputs = tokens.astype(jnp.float32).reshape(groups, TOK_GRP, D)
    grads_in = out_grad.astype(jnp.float32).reshape(groups, TOK_GRP, D)

    def one_group(totals, item):
        rows, cotangent = item
        result, pull = jax.vjp(group_forward, params, rows)
        grad_params, grad_rows = pull(cotangent)
        totals = jax.tree.map(jnp.add, totals, grad_params)
        return (totals, (result, grad_rows))
    zeros = jax.tree.map(jnp.zeros_like, params)
    totals, (results, grad_rows) = lax.scan(one_group, zeros, (inputs, grads_in))
    return (results.reshape(TOKENS, D), grad_rows.reshape(TOKENS, D), totals[0], totals[1], totals[2], totals[3], totals[4], totals[5], totals[6], totals[7], totals[8], totals[9], totals[10], totals[11])
```

```python
import jax
import jax.numpy as jnp
from jax import lax
from jax.experimental import pallas as pl
from jax.experimental.pallas import tpu as pltpu
from jax.sharding import PartitionSpec as P

HD = 64
LEN = 1024


EPS = 1e-05
NEG = -1e30
BLOCK = 256
BF = jnp.bfloat16
F32 = jnp.float32


def dot(left, right, dims):
    return lax.dot_general(left, right, (dims, ((), ())), preferred_element_type=F32)


def mm(left, right):
    return dot(left, right, ((1,), (0,)))


def mm_t(left, right):
    return dot(left, right, ((1,), (1,)))


def t_mm(left, right):
    return dot(left, right, ((0,), (0,)))


def layer_norm(values, gain, bias):
    center = values - jnp.mean(values, -1, keepdims=True)
    spread = jnp.mean(center * center, -1, keepdims=True)
    return center * lax.rsqrt(spread + EPS) * gain + bias


def gelu_tanh(values):
    return jax.nn.gelu(values, approximate=True)


def swap(value, bit):
    size = lax.axis_size("tensor")
    return lax.ppermute(value, "tensor", [(i, i ^ bit) for i in range(size)])


def after(value, *others):
    return lax.optimization_barrier((value,) + others)[0]


def chunk_count():
    size = lax.axis_size("tensor")
    return 4 if size == 4 else 1


def gather_rows(local):
    if chunk_count() == 1:
        return [lax.all_gather(local, "tensor", axis=0, tiled=True)]
    sib = swap(local, 1)
    far = swap(local, 2)
    return [local, sib, far, swap(far, 1)]


def sum_rows(part):
    if chunk_count() == 1:
        return lax.psum_scatter(part(0), "tensor", scatter_dimension=0, tiled=True)
    side = swap(part(3).astype(BF), 1)
    cross = swap((part(2) + side.astype(F32)).astype(BF), 2)
    near = swap(part(1).astype(BF), 1)
    return part(0) + near.astype(F32) + cross.astype(F32)


def take_rows(full, k):
    if chunk_count() == 1:
        return full
    rows = full.shape[0] // 4
    return lax.dynamic_slice_in_dim(full, (lax.axis_index("tensor") ^ k) * rows, rows, 0)


def in_order(pieces):
    if len(pieces) == 1:
        return pieces[0]
    rows = pieces[0].shape[0]
    me = lax.axis_index("tensor")
    full = jnp.zeros((4 * rows, pieces[0].shape[1]), pieces[0].dtype)
    for k, piece in enumerate(pieces):
        full = lax.dynamic_update_slice_in_dim(full, piece, (me ^ k) * rows, 0)
    return full


def joined_rows(pieces):
    return pieces[0] if len(pieces) == 1 else jnp.concatenate(pieces, 0)


def replica_sum(value):
    size = lax.axis_size("replica")
    if size == 2:
        return value.astype(F32) + lax.ppermute(value, "replica", [(0, 1), (1, 0)]).astype(F32)
    return lax.psum(value, "replica").astype(F32)


def scores_t(qkv_ref, width, head, block):
    stop = (block + 1) * BLOCK
    low = head * HD
    query = qkv_ref[block * BLOCK : stop, low : low + HD]
    keys = qkv_ref[0:stop, width + low : width + low + HD]
    scores = mm_t(keys, query * jnp.asarray(HD ** (-0.5), BF))
    shape = (BLOCK, BLOCK)
    keep = lax.broadcasted_iota(jnp.int32, shape, 0) <= lax.broadcasted_iota(jnp.int32, shape, 1)
    edge = jnp.where(keep, scores[stop - BLOCK :], NEG)
    scores = edge if block == 0 else jnp.concatenate([scores[: stop - BLOCK], edge], 0)
    expo = jnp.exp(scores - jnp.max(scores, 0, keepdims=True))
    return query, keys, expo, 1.0 / jnp.sum(expo, 0, keepdims=True)


def attend_kernel(qkv_ref, out_ref):
    width = out_ref.shape[1]
    for pair in range(width // (2 * HD)):
        for block in range(LEN // BLOCK):
            stop = (block + 1) * BLOCK
            halves = []
            for head in (2 * pair, 2 * pair + 1):
                _, _, expo, inverse = scores_t(qkv_ref, width, head, block)
                low = 2 * width + head * HD
                values = qkv_ref[0:stop, low : low + HD]
                halves.append(t_mm(values, expo.astype(BF)) * inverse)
            out_ref[block * BLOCK : stop, pair * 2 * HD : (pair + 1) * 2 * HD] = (
                jnp.concatenate(halves, 0).T.astype(BF)
            )


def attend_back_kernel(qkv_ref, grad_ref, out_ref, keys_sum, values_sum):
    width = grad_ref.shape[1]
    scale = HD ** (-0.5)
    for pair in range(width // (2 * HD)):
        for block in reversed(range(LEN // BLOCK)):
            stop = (block + 1) * BLOCK
            halves = []
            for side in (0, 1):
                head = 2 * pair + side
                query, keys, expo, inverse = scores_t(qkv_ref, width, head, block)
                low = head * HD
                values = qkv_ref[0:stop, 2 * width + low : 2 * width + low + HD]
                grad = grad_ref[block * BLOCK : stop, low : low + HD]
                probs = expo * inverse
                grad_values = mm(probs.astype(BF), grad)
                grad_probs = mm_t(values, grad)
                weighted = probs * grad_probs
                total = jnp.sum(weighted, 0, keepdims=True)
                grad_scores = (weighted - probs * total).astype(BF)
                grad_keys = mm(grad_scores, query)
                lanes = slice(side * HD, (side + 1) * HD)
                if stop == LEN:
                    values_sum[:, lanes] = grad_values
                    keys_sum[:, lanes] = grad_keys
                else:
                    values_sum[0:stop, lanes] += grad_values
                    keys_sum[0:stop, lanes] += grad_keys
                halves.append(t_mm(keys, grad_scores))
            low = pair * 2 * HD
            out_ref[block * BLOCK : stop, low : low + 2 * HD] = (
                jnp.concatenate(halves, 0).T * scale
            ).astype(BF)
        out_ref[:, width + low : width + low + 2 * HD] = (keys_sum[...] * scale).astype(BF)
        out_ref[:, 2 * width + low : 2 * width + low + 2 * HD] = values_sum[...].astype(BF)


def rows_spec(width):
    return pl.BlockSpec((LEN, width), lambda i: (i, 0))


def attend(qkv):
    rows, width = qkv.shape[0], qkv.shape[1] // 3
    return pl.pallas_call(
        attend_kernel,
        grid=(rows // LEN,),
        in_specs=[rows_spec(3 * width)],
        out_specs=rows_spec(width),
        out_shape=jax.ShapeDtypeStruct((rows, width), BF),
        cost_estimate=pl.CostEstimate(
            flops=24_000_000_000, bytes_accessed=8 * rows * width, transcendentals=rows * width * 4
        ),
        compiler_params=pltpu.CompilerParams(vmem_limit_bytes=48 * 1024 * 1024),
        name="attend",
    )(qkv)


def attend_back(qkv, grad):
    rows, width = grad.shape
    return pl.pallas_call(
        attend_back_kernel,
        grid=(rows // LEN,),
        in_specs=[rows_spec(3 * width), rows_spec(width)],
        out_specs=rows_spec(3 * width),
        out_shape=jax.ShapeDtypeStruct((rows, 3 * width), BF),
        scratch_shapes=[pltpu.VMEM((LEN, 2 * HD), F32), pltpu.VMEM((LEN, 2 * HD), F32)],
        cost_estimate=pl.CostEstimate(
            flops=48_000_000_000, bytes_accessed=14 * rows * width, transcendentals=rows * width * 4
        ),
        compiler_params=pltpu.CompilerParams(vmem_limit_bytes=48 * 1024 * 1024),
        name="attend_back",
    )(qkv, grad)


def pack(flat):
    size = flat.shape[-1]
    full = -(-size // 1024) * 1024
    flat = jnp.pad(flat, [(0, 0)] * (flat.ndim - 1) + [(0, full - size)])
    return flat.reshape(flat.shape[:-1] + (full // 128, 128))


def on_device_wide(
    tokens,
    ln1_gain,
    ln1_bias,
    qkv_weight,
    qv_bias,
    out_weight,
    out_bias,
    ln2_gain,
    ln2_bias,
    fc_weight,
    fc_bias,
    proj_weight,
    proj_bias,
    out_grad,
):
    both = ("fsdp", "tensor")
    n_fsdp, n_tensor = lax.axis_size("fsdp"), lax.axis_size("tensor")
    me = lax.axis_index("tensor")
    part = ln1_gain.shape[0]
    width = out_weight.shape[0]
    heads = width // HD
    hidden = fc_weight.shape[1]
    model = tokens.shape[1]
    vectors = jnp.concatenate(
        [
            ln1_gain,
            ln1_bias,
            ln2_gain,
            ln2_bias,
            out_bias,
            proj_bias,
            qv_bias.astype(F32).reshape(-1),
            fc_bias.astype(F32).reshape(-1),
        ]
    )
    bundle = lax.all_gather(pack(vectors), both, axis=0, tiled=False)
    bundle = bundle.reshape(n_fsdp * n_tensor, -1)
    gain_one, bias_one, gain_two, bias_two, bias_out, bias_proj = (
        bundle[:, i * part : (i + 1) * part].reshape(-1) for i in range(6)
    )
    mine = lax.dynamic_index_in_dim(bundle.reshape(n_fsdp, n_tensor, -1), me, 1, keepdims=False)
    low, high = 6 * part, 6 * part + qv_bias.size
    qv_full = (
        mine[:, low:high].reshape((n_fsdp,) + qv_bias.shape).transpose(1, 2, 0, 3).reshape(2, width)
    )
    fcb_full = (
        mine[:, high : high + fc_bias.size]
        .reshape((n_fsdp,) + fc_bias.shape)
        .transpose(1, 0, 2)
        .reshape(hidden)
    )
    bias_row = jnp.concatenate([qv_full[0], jnp.zeros((width,), F32), qv_full[1]])
    joined = lax.all_gather(
        qkv_weight.reshape(qkv_weight.shape[0], 3 * width), "fsdp", axis=0, tiled=True
    )
    out_full = lax.all_gather(out_weight, "fsdp", axis=1, tiled=True)
    fc_full = lax.all_gather(fc_weight, "fsdp", axis=0, tiled=True)
    proj_full = lax.all_gather(proj_weight, "fsdp", axis=1, tiled=True)

    inputs = tokens.astype(F32)
    normed_one = gather_rows(layer_norm(inputs, gain_one, bias_one).astype(BF))
    qkv = in_order([(mm(piece, joined) + bias_row).astype(BF) for piece in normed_one])
    attended = attend(qkv)
    att = [take_rows(attended, k) for k in range(chunk_count())]
    grads = gather_rows(after(out_grad, qkv))
    middle = inputs + (sum_rows(lambda k: mm(att[k], out_full)) + bias_out)
    normed_two = gather_rows(layer_norm(middle, gain_two, bias_two).astype(BF))
    before = [mm(piece, fc_full) + fcb_full for piece in normed_two]
    act = [gelu_tanh(piece).astype(BF) for piece in before]

    grad_pre = []
    for piece, grad in zip(before, grads):
        pull = jax.vjp(gelu_tanh, piece)[1]
        grad_pre.append(pull(mm_t(grad, proj_full))[0].astype(BF))
    grad_normed_two = sum_rows(lambda k: mm_t(grad_pre[k], fc_full))
    grad_pre_all = joined_rows(grad_pre)
    grad_proj = t_mm(joined_rows(act), joined_rows(grads)).astype(BF)
    grad_fc = t_mm(joined_rows(normed_two), grad_pre_all).astype(BF)
    grad_fc_bias = jnp.sum(grad_pre_all, 0, dtype=F32)
    grad_proj_bias = jnp.sum(out_grad, 0, dtype=F32)
    norm_pull_two = jax.vjp(layer_norm, middle, gain_two, bias_two)[1]
    grad_middle_part, grad_gain_two, grad_bias_two = norm_pull_two(grad_normed_two)
    grad_middle = out_grad.astype(F32) + grad_middle_part
    grad_branch = grad_middle.astype(BF)
    grad_out_bias = jnp.sum(grad_branch, 0, dtype=F32)
    branches = gather_rows(grad_branch)
    grad_attended = in_order([mm_t(piece, out_full).astype(BF) for piece in branches])

    late = lax.optimization_barrier((grad_attended, *act))
    grad_attended, act = late[0], late[1:]
    output = middle + sum_rows(lambda k: mm(act[k], proj_full)) + bias_proj
    grad_qkv = attend_back(qkv, grad_attended)
    grad_out = t_mm(joined_rows(att), joined_rows(branches)).astype(BF)
    pieces = [take_rows(grad_qkv, k) for k in range(chunk_count())]
    grad_normed_one = sum_rows(lambda k: mm_t(pieces[k], joined))
    pieces_all = joined_rows(pieces)
    grad_joined = t_mm(joined_rows(normed_one), pieces_all).astype(BF)
    qkv_sums = jnp.sum(pieces_all, 0, dtype=F32)
    norm_pull_one = jax.vjp(layer_norm, inputs, gain_one, bias_one)[1]
    grad_input_part, grad_gain_one, grad_bias_one = norm_pull_one(grad_normed_one)
    input_grad = grad_middle + grad_input_part

    def scatter(value, dim):
        return replica_sum(
            lax.psum_scatter(value, "fsdp", scatter_dimension=dim, tiled=True).astype(BF)
        )

    total_proj = scatter(grad_proj, 1)
    total_fc = scatter(grad_fc, 0)
    total_out = scatter(grad_out, 1)
    total_joined = scatter(grad_joined, 0)

    wide = jnp.stack(
        [grad_gain_one, grad_bias_one, grad_gain_two, grad_bias_two, grad_out_bias, grad_proj_bias]
    )
    wide = wide.reshape(6, n_fsdp * n_tensor, part).transpose(1, 0, 2).reshape(-1, 6 * part)
    grad_qv = jnp.stack([qkv_sums[:width], qkv_sums[2 * width :]])
    grad_qv = grad_qv.reshape(2, heads, n_fsdp, -1).transpose(2, 0, 1, 3).reshape(n_fsdp, -1)
    grad_fcb = grad_fc_bias.reshape(fc_bias.shape[0], n_fsdp, -1).transpose(1, 0, 2)
    own = jnp.concatenate([grad_qv, grad_fcb.reshape(n_fsdp, -1)], -1)
    is_me = (jnp.arange(n_tensor, dtype=jnp.int32) == me)[None, :, None]
    own = jnp.where(is_me, own[:, None, :], 0.0).reshape(n_fsdp * n_tensor, -1)
    sums = lax.psum_scatter(
        pack(jnp.concatenate([wide, own], -1)), both, scatter_dimension=0, tiled=False
    )
    sums = replica_sum(sums).reshape(-1)
    vec = [sums[i * part : (i + 1) * part] for i in range(6)]
    total_qv = sums[low:high].reshape(qv_bias.shape)
    total_fcb = sums[high : high + fc_bias.size].reshape(fc_bias.shape)
    return (
        output,
        input_grad,
        vec[0],
        vec[1],
        total_joined.reshape(qkv_weight.shape),
        total_qv,
        total_out,
        vec[4],
        vec[2],
        vec[3],
        total_fc,
        total_fcb,
        total_proj,
        vec[5],
    )


MESH = pl.DeviceIdType.MESH
HALF = LEN // 2


def chip_swap(value):
    return swap(value, 2)


def y_swap(value):
    return lax.ppermute(value, "replica", [(0, 1), (1, 0)])


def put(full, piece, row, column=0):
    return lax.dynamic_update_slice(full, piece, (row, jnp.int32(column)))


def rows_at(full, row, count):
    return lax.dynamic_slice_in_dim(full, row, count, 0)


def two(first, second, index):
    low, high = jnp.concatenate([first, second], 0), jnp.concatenate([second, first], 0)
    return jnp.where(index == 0, low, high)


def other_chip(native):
    y = lax.axis_index("replica")
    half = native.shape[0] // 2
    near = chip_swap(rows_at(native, y * half, half))
    return two(near, y_swap(near), y)


def group_peer(step):
    n_fsdp, n_tensor = lax.axis_size("fsdp"), lax.axis_size("tensor")
    size = n_fsdp * n_tensor
    me = lax.axis_index("fsdp") * n_tensor + lax.axis_index("tensor")
    peer = lax.rem(me + step, size)
    place = (lax.axis_index("replica"), peer // n_tensor, lax.rem(peer, n_tensor))
    return me, peer, place


def greet(size):
    barrier = pltpu.get_barrier_semaphore()
    for step in range(1, size):
        pl.semaphore_signal(
            barrier, inc=1, device_id=group_peer(step)[2], device_id_type=MESH
        )
    pl.semaphore_wait(barrier, size - 1)


def small_gather_kernel(in_ref, out_ref, send, recv):
    size = out_ref.shape[0]
    greet(size)
    copies = []
    for step in range(1, size):
        me, _, place = group_peer(step)
        copy = pltpu.make_async_remote_copy(
            src_ref=in_ref,
            dst_ref=out_ref.at[me],
            send_sem=send.at[step],
            recv_sem=recv.at[step],
            device_id=place,
            device_id_type=MESH,
        )
        copy.start()
        copies.append(copy)
    out_ref[group_peer(0)[0]] = in_ref[...]
    for copy in copies:
        copy.wait()


def small_scatter_kernel(in_ref, out_ref, held, send, recv):
    size = in_ref.shape[0]
    greet(size)
    copies = []
    for step in range(1, size):
        _, peer, place = group_peer(step)
        copy = pltpu.make_async_remote_copy(
            src_ref=in_ref.at[peer],
            dst_ref=held.at[step],
            send_sem=send.at[step],
            recv_sem=recv.at[step],
            device_id=place,
            device_id_type=MESH,
        )
        copy.start()
        copies.append(copy)
    total = in_ref[group_peer(0)[0]]
    for step, copy in enumerate(copies):
        copy.wait()
        total = total + held[step + 1]
    out_ref[...] = total


def small_gather(value, size):
    return pl.pallas_call(
        small_gather_kernel,
        in_specs=[pl.BlockSpec(memory_space=pltpu.VMEM)],
        out_specs=pl.BlockSpec(memory_space=pltpu.VMEM),
        out_shape=jax.ShapeDtypeStruct((size,) + value.shape, F32),
        scratch_shapes=[pltpu.SemaphoreType.DMA((size,)), pltpu.SemaphoreType.DMA((size,))],
        compiler_params=pltpu.CompilerParams(collective_id=1, has_side_effects=True),
        name="small_gather",
    )(value)


def small_scatter(value):
    size = value.shape[0]
    return pl.pallas_call(
        small_scatter_kernel,
        in_specs=[pl.BlockSpec(memory_space=pltpu.VMEM)],
        out_specs=pl.BlockSpec(memory_space=pltpu.VMEM),
        out_shape=jax.ShapeDtypeStruct(value.shape[1:], F32),
        scratch_shapes=[
            pltpu.VMEM(value.shape, F32),
            pltpu.SemaphoreType.DMA((size,)),
            pltpu.SemaphoreType.DMA((size,)),
        ],
        compiler_params=pltpu.CompilerParams(collective_id=2, has_side_effects=True),
        name="small_scatter",
    )(value)


def attend_own_kernel(qkv_ref, out_ref):
    start = pl.multiple_of((lax.axis_index("tensor") // 2) * HALF, HALF)
    attend_kernel(qkv_ref.at[pl.ds(start, LEN)], out_ref)


def attend_back_own_kernel(qkv_ref, grad_ref, out_ref, keys_sum, values_sum):
    start = pl.multiple_of((lax.axis_index("tensor") // 2) * HALF, HALF)
    rows = pl.ds(start, LEN)
    attend_back_kernel(qkv_ref.at[rows], grad_ref.at[rows], out_ref, keys_sum, values_sum)


def attend_own(qkv):
    rows, width = qkv.shape[0], qkv.shape[1] // 6
    return pl.pallas_call(
        attend_own_kernel,
        grid=(2,),
        in_specs=[pl.BlockSpec((rows, 3 * width), lambda i: (0, i))],
        out_specs=pl.BlockSpec((LEN, width), lambda i: (0, i)),
        out_shape=jax.ShapeDtypeStruct((LEN, 2 * width), BF),
        cost_estimate=pl.CostEstimate(
            flops=16_000_000_000, bytes_accessed=20 * LEN * width, transcendentals=8 * LEN * width
        ),
        compiler_params=pltpu.CompilerParams(vmem_limit_bytes=48 * 1024 * 1024),
        name="attend_own",
    )(qkv)


def attend_back_own(qkv, grad):
    rows, width = qkv.shape[0], qkv.shape[1] // 6
    return pl.pallas_call(
        attend_back_own_kernel,
        grid=(2,),
        in_specs=[
            pl.BlockSpec((rows, 3 * width), lambda i: (0, i)),
            pl.BlockSpec((rows, width), lambda i: (0, i)),
        ],
        out_specs=pl.BlockSpec((LEN, 3 * width), lambda i: (0, i)),
        out_shape=jax.ShapeDtypeStruct((LEN, 6 * width), BF),
        scratch_shapes=[pltpu.VMEM((LEN, 2 * HD), F32), pltpu.VMEM((LEN, 2 * HD), F32)],
        cost_estimate=pl.CostEstimate(
            flops=32_000_000_000, bytes_accessed=32 * LEN * width, transcendentals=8 * LEN * width
        ),
        compiler_params=pltpu.CompilerParams(vmem_limit_bytes=48 * 1024 * 1024),
        name="attend_back_own",
    )(qkv, grad)


def on_device_chip(
    tokens,
    ln1_gain,
    ln1_bias,
    qkv_weight,
    qv_bias,
    out_weight,
    out_bias,
    ln2_gain,
    ln2_bias,
    fc_weight,
    fc_bias,
    proj_weight,
    proj_bias,
    out_grad,
):
    n_fsdp, n_tensor = lax.axis_size("fsdp"), lax.axis_size("tensor")
    group = n_fsdp * n_tensor
    me = lax.axis_index("tensor")
    x, core = me // 2, me % 2
    part = ln1_gain.shape[0]
    width = out_weight.shape[0]
    heads = width // HD
    hidden = fc_weight.shape[1]
    rows, model = tokens.shape
    mid_row = (1 - x) * LEN
    own_row = x * HALF
    row_of = (core * rows, (1 - core) * rows)

    vectors = jnp.concatenate(
        [
            ln1_gain,
            ln1_bias,
            ln2_gain,
            ln2_bias,
            out_bias,
            proj_bias,
            qv_bias.astype(F32).reshape(-1),
            fc_bias.astype(F32).reshape(-1),
        ]
    )
    bundle = small_gather(pack(vectors), group).reshape(group, -1)
    gain_one, bias_one, gain_two, bias_two, bias_out, bias_proj = (
        bundle[:, i * part : (i + 1) * part].reshape(-1) for i in range(6)
    )
    by_tensor = bundle.reshape(n_fsdp, n_tensor, -1)
    low, high = 6 * part, 6 * part + qv_bias.size
    bias_rows, fcb_rows = [], []
    for place in (me, me ^ 2):
        mine = lax.dynamic_index_in_dim(by_tensor, place, 1, keepdims=False)
        qv = (
            mine[:, low:high]
            .reshape((n_fsdp,) + qv_bias.shape)
            .transpose(1, 2, 0, 3)
            .reshape(2, width)
        )
        bias_rows.append(jnp.concatenate([qv[0], jnp.zeros((width,), F32), qv[1]]))
        fcb_rows.append(
            mine[:, high : high + fc_bias.size]
            .reshape((n_fsdp,) + fc_bias.shape)
            .transpose(1, 0, 2)
            .reshape(hidden)
        )
    fcb_full = jnp.concatenate(fcb_rows)

    joined_near = lax.all_gather(
        qkv_weight.reshape(qkv_weight.shape[0], 3 * width), "fsdp", axis=0, tiled=True
    )
    joined = [joined_near, other_chip(joined_near)]
    out_near = lax.all_gather(out_weight, "fsdp", axis=1, tiled=True)
    out_full = jnp.concatenate([out_near, other_chip(out_near)], 0)
    fc_near = lax.all_gather(fc_weight, "fsdp", axis=0, tiled=True)
    fc_full = jnp.concatenate([fc_near, other_chip(fc_near)], 1)
    proj_near = lax.all_gather(proj_weight, "fsdp", axis=1, tiled=True)
    proj_full = jnp.concatenate([proj_near, other_chip(proj_near)], 0)

    def pair(local):
        return [local, swap(local, 1)]

    def pair_sum(term):
        side = swap(term(1).astype(BF), 1)
        return term(0) + side.astype(F32)

    inputs = tokens.astype(F32)
    normed_one = pair(layer_norm(inputs, gain_one, bias_one).astype(BF))
    qkv = jnp.zeros((2 * rows, 6 * width), BF)
    for j in range(2):
        for k in range(2):
            piece = (mm(normed_one[k], joined[j]) + bias_rows[j]).astype(BF)
            qkv = put(qkv, piece, row_of[k], 3 * width * j)
    qkv_mid_half = rows_at(qkv, mid_row, HALF)
    mid_far = chip_swap(qkv_mid_half[:, 3 * width :])
    att_own = attend_own(qkv)
    qkv_mid = two(qkv_mid_half[:, : 3 * width], mid_far, x)
    att_mid = attend(qkv_mid)
    att_far = chip_swap(rows_at(att_mid, (1 - x) * HALF, HALF))
    attended = jnp.zeros((2 * rows, 2 * width), BF)
    attended = put(attended, att_own, own_row)
    attended = put(attended, rows_at(att_mid, x * HALF, HALF), mid_row)
    attended = put(attended, att_far, mid_row, width)
    att = [rows_at(attended, row_of[k], rows) for k in range(2)]
    grads = pair(after(out_grad, qkv))
    middle = inputs + (pair_sum(lambda k: mm(att[k], out_full)) + bias_out)
    normed_two = pair(layer_norm(middle, gain_two, bias_two).astype(BF))
    before = [mm(piece, fc_full) + fcb_full for piece in normed_two]
    act = [gelu_tanh(piece).astype(BF) for piece in before]

    grad_pre = []
    for piece, grad in zip(before, grads):
        pull = jax.vjp(gelu_tanh, piece)[1]
        grad_pre.append(pull(mm_t(grad, proj_full))[0].astype(BF))
    grad_normed_two = pair_sum(lambda k: mm_t(grad_pre[k], fc_full))
    grad_pre_all = joined_rows(grad_pre)
    grad_proj = t_mm(joined_rows(act), joined_rows(grads)).astype(BF)
    grad_fc = t_mm(joined_rows(normed_two), grad_pre_all).astype(BF)
    grad_fc_bias = jnp.sum(grad_pre_all, 0, dtype=F32)
    grad_proj_bias = jnp.sum(out_grad, 0, dtype=F32)
    norm_pull_two = jax.vjp(layer_norm, middle, gain_two, bias_two)[1]
    grad_middle_part, grad_gain_two, grad_bias_two = norm_pull_two(grad_normed_two)
    grad_middle = out_grad.astype(F32) + grad_middle_part
    grad_branch = grad_middle.astype(BF)
    grad_out_bias = jnp.sum(grad_branch, 0, dtype=F32)
    branches = pair(grad_branch)
    grad_attended = jnp.zeros((2 * rows, 2 * width), BF)
    for k in range(2):
        grad_attended = put(grad_attended, mm_t(branches[k], out_full).astype(BF), row_of[k])

    grad_mid_half = rows_at(grad_attended, mid_row, HALF)
    grad_mid_far = chip_swap(grad_mid_half[:, width:])
    late = lax.optimization_barrier((grad_attended, *act))
    grad_attended, act = late[0], late[1:]
    output = middle + pair_sum(lambda k: mm(act[k], proj_full)) + bias_proj
    grad_mid = two(grad_mid_half[:, :width], grad_mid_far, x)
    back_mid = attend_back(qkv_mid, grad_mid)
    back_far = chip_swap(rows_at(back_mid, (1 - x) * HALF, HALF))
    back_own = attend_back_own(qkv, after(grad_attended, back_mid))
    grad_out = t_mm(joined_rows(att), joined_rows(branches)).astype(BF)
    grad_qkv = jnp.zeros((2 * rows, 6 * width), BF)
    grad_qkv = put(grad_qkv, back_own, own_row)
    grad_qkv = put(grad_qkv, rows_at(back_mid, x * HALF, HALF), mid_row)
    grad_qkv = put(grad_qkv, back_far, mid_row, 3 * width)
    pieces = [rows_at(grad_qkv, row_of[k], rows) for k in range(2)]
    cut = 3 * width
    pieces_all = joined_rows(pieces)
    normed_all = joined_rows(normed_one)
    grad_joined = [
        t_mm(normed_all, pieces_all[:, j * cut : (j + 1) * cut]).astype(BF) for j in range(2)
    ]
    qkv_sums = jnp.sum(pieces_all, 0, dtype=F32)
    joined_both = jnp.concatenate(joined, 1)
    grad_normed_one = pair_sum(lambda k: mm_t(pieces[k], joined_both))
    norm_pull_one = jax.vjp(layer_norm, inputs, gain_one, bias_one)[1]
    grad_input_part, grad_gain_one, grad_bias_one = norm_pull_one(grad_normed_one)
    input_grad = grad_middle + grad_input_part

    def scatter(near, far, dim):
        both = (near.astype(F32) + chip_swap(far).astype(F32)).astype(BF)
        return replica_sum(
            lax.psum_scatter(both, "fsdp", scatter_dimension=dim, tiled=True).astype(BF)
        )

    total_proj = scatter(grad_proj[:hidden], grad_proj[hidden:], 1)
    total_fc = scatter(grad_fc[:, :hidden], grad_fc[:, hidden:], 0)
    total_out = scatter(grad_out[:width], grad_out[width:], 1)
    total_joined = scatter(grad_joined[0], grad_joined[1], 0)

    wide = jnp.stack(
        [grad_gain_one, grad_bias_one, grad_gain_two, grad_bias_two, grad_out_bias, grad_proj_bias]
    )
    wide = wide.reshape(6, group, part).transpose(1, 0, 2).reshape(-1, 6 * part)
    own = []
    for j in range(2):
        sums = qkv_sums[j * cut : (j + 1) * cut]
        grad_qv = jnp.stack([sums[:width], sums[2 * width :]])
        grad_qv = grad_qv.reshape(2, heads, n_fsdp, -1).transpose(2, 0, 1, 3).reshape(n_fsdp, -1)
        grad_fcb = grad_fc_bias[j * hidden : (j + 1) * hidden]
        grad_fcb = grad_fcb.reshape(fc_bias.shape[0], n_fsdp, -1).transpose(1, 0, 2)
        own.append(jnp.concatenate([grad_qv, grad_fcb.reshape(n_fsdp, -1)], -1))
    index = jnp.arange(n_tensor, dtype=jnp.int32)[None, :, None]
    own = jnp.where(
        index == me, own[0][:, None, :], jnp.where(index == (me ^ 2), own[1][:, None, :], 0.0)
    ).reshape(group, -1)
    sums = replica_sum(small_scatter(pack(jnp.concatenate([wide, own], -1)))).reshape(-1)
    vec = [sums[i * part : (i + 1) * part] for i in range(6)]
    total_qv = sums[low:high].reshape(qv_bias.shape)
    total_fcb = sums[high : high + fc_bias.size].reshape(fc_bias.shape)
    return (
        output,
        input_grad,
        vec[0],
        vec[1],
        total_joined.reshape(qkv_weight.shape),
        total_qv,
        total_out,
        vec[4],
        vec[2],
        vec[3],
        total_fc,
        total_fcb,
        total_proj,
        vec[5],
    )


def on_device(*arrays):
    pairs = lax.axis_size("tensor") == 4 and lax.axis_size("replica") == 2
    if pairs and 2 * arrays[0].shape[0] == LEN + HALF:
        return on_device_chip(*arrays)
    return on_device_wide(*arrays)


def solution(mesh):
    placed = (
        P(("replica", "fsdp", "tensor"), None),
        P(("fsdp", "tensor")),
        P(("fsdp", "tensor")),
        P("fsdp", None, "tensor"),
        P(None, "tensor", "fsdp"),
        P("tensor", "fsdp"),
        P(("fsdp", "tensor")),
        P(("fsdp", "tensor")),
        P(("fsdp", "tensor")),
        P("fsdp", "tensor"),
        P("tensor", "fsdp"),
        P("tensor", "fsdp"),
        P(("fsdp", "tensor")),
        P(("replica", "fsdp", "tensor"), None),
    )
    return jax.shard_map(
        on_device,
        mesh=mesh,
        in_specs=placed,
        out_specs=(
            P(("replica", "fsdp", "tensor"), None),
            P(("replica", "fsdp", "tensor"), None),
            P(("fsdp", "tensor")),
            P(("fsdp", "tensor")),
            P("fsdp", None, "tensor"),
            P(None, "tensor", "fsdp"),
            P("tensor", "fsdp"),
            P(("fsdp", "tensor")),
            P(("fsdp", "tensor")),
            P(("fsdp", "tensor")),
            P("fsdp", "tensor"),
            P("tensor", "fsdp"),
            P("tensor", "fsdp"),
            P(("fsdp", "tensor")),
        ),
        check_vma=False,
    )
```

```python
import jax
import jax.numpy as jnp
from jax import lax
from jax.experimental import pallas as pl
from jax.experimental.pallas import tpu as pltpu
from jax.sharding import PartitionSpec as P

HD = 64
LEN = 1024


EPS = 1e-05
NEG = -1e30
BLOCK = 256
BF = jnp.bfloat16
F32 = jnp.float32


def dot(left, right, dims):
    return lax.dot_general(left, right, (dims, ((), ())), preferred_element_type=F32)


def mm(left, right):
    return dot(left, right, ((1,), (0,)))


def mm_t(left, right):
    return dot(left, right, ((1,), (1,)))


def t_mm(left, right):
    return dot(left, right, ((0,), (0,)))


def layer_norm(values, gain, bias):
    center = values - jnp.mean(values, -1, keepdims=True)
    spread = jnp.mean(center * center, -1, keepdims=True)
    return center * lax.rsqrt(spread + EPS) * gain + bias


def gelu_tanh(values):
    return jax.nn.gelu(values, approximate=True)


def swap(value, bit):
    size = lax.axis_size("tensor")
    return lax.ppermute(value, "tensor", [(i, i ^ bit) for i in range(size)])


def after(value, *others):
    return lax.optimization_barrier((value,) + others)[0]


def chunk_count():
    size = lax.axis_size("tensor")
    return 4 if size == 4 else 1


def gather_rows(local):
    if chunk_count() == 1:
        return [lax.all_gather(local, "tensor", axis=0, tiled=True)]
    sib = swap(local, 1)
    far = swap(local, 2)
    return [local, sib, far, swap(far, 1)]


def sum_rows(part):
    if chunk_count() == 1:
        return lax.psum_scatter(part(0), "tensor", scatter_dimension=0, tiled=True)
    side = swap(part(3).astype(BF), 1)
    cross = swap((part(2) + side.astype(F32)).astype(BF), 2)
    near = swap(part(1).astype(BF), 1)
    return part(0) + near.astype(F32) + cross.astype(F32)


def take_rows(full, k):
    if chunk_count() == 1:
        return full
    rows = full.shape[0] // 4
    return lax.dynamic_slice_in_dim(full, (lax.axis_index("tensor") ^ k) * rows, rows, 0)


def in_order(pieces):
    if len(pieces) == 1:
        return pieces[0]
    rows = pieces[0].shape[0]
    me = lax.axis_index("tensor")
    full = jnp.zeros((4 * rows, pieces[0].shape[1]), pieces[0].dtype)
    for k, piece in enumerate(pieces):
        full = lax.dynamic_update_slice_in_dim(full, piece, (me ^ k) * rows, 0)
    return full


def joined_rows(pieces):
    return pieces[0] if len(pieces) == 1 else jnp.concatenate(pieces, 0)


def replica_sum(value):
    size = lax.axis_size("replica")
    if size == 2:
        return value.astype(F32) + lax.ppermute(value, "replica", [(0, 1), (1, 0)]).astype(F32)
    return lax.psum(value, "replica").astype(F32)


def scores_t(qkv_ref, width, head, block):
    stop = (block + 1) * BLOCK
    low = head * HD
    query = qkv_ref[block * BLOCK : stop, low : low + HD]
    keys = qkv_ref[0:stop, width + low : width + low + HD]
    scores = mm_t(keys, query * jnp.asarray(HD ** (-0.5), BF))
    shape = (BLOCK, BLOCK)
    keep = lax.broadcasted_iota(jnp.int32, shape, 0) <= lax.broadcasted_iota(jnp.int32, shape, 1)
    edge = jnp.where(keep, scores[stop - BLOCK :], NEG)
    scores = edge if block == 0 else jnp.concatenate([scores[: stop - BLOCK], edge], 0)
    expo = jnp.exp(scores - jnp.max(scores, 0, keepdims=True))
    return query, keys, expo, 1.0 / jnp.sum(expo, 0, keepdims=True)


def attend_kernel(qkv_ref, out_ref):
    width = out_ref.shape[1]
    for pair in range(width // (2 * HD)):
        for block in range(LEN // BLOCK):
            stop = (block + 1) * BLOCK
            halves = []
            for head in (2 * pair, 2 * pair + 1):
                _, _, expo, inverse = scores_t(qkv_ref, width, head, block)
                low = 2 * width + head * HD
                values = qkv_ref[0:stop, low : low + HD]
                halves.append(t_mm(values, expo.astype(BF)) * inverse)
            out_ref[block * BLOCK : stop, pair * 2 * HD : (pair + 1) * 2 * HD] = (
                jnp.concatenate(halves, 0).T.astype(BF)
            )


def attend_back_kernel(qkv_ref, grad_ref, out_ref, keys_sum, values_sum):
    width = grad_ref.shape[1]
    scale = HD ** (-0.5)
    for pair in range(width // (2 * HD)):
        for block in reversed(range(LEN // BLOCK)):
            stop = (block + 1) * BLOCK
            halves = []
            for side in (0, 1):
                head = 2 * pair + side
                query, keys, expo, inverse = scores_t(qkv_ref, width, head, block)
                low = head * HD
                values = qkv_ref[0:stop, 2 * width + low : 2 * width + low + HD]
                grad = grad_ref[block * BLOCK : stop, low : low + HD]
                probs = expo * inverse
                grad_values = mm(probs.astype(BF), grad)
                grad_probs = mm_t(values, grad)
                weighted = probs * grad_probs
                total = jnp.sum(weighted, 0, keepdims=True)
                grad_scores = (weighted - probs * total).astype(BF)
                grad_keys = mm(grad_scores, query)
                lanes = slice(side * HD, (side + 1) * HD)
                if stop == LEN:
                    values_sum[:, lanes] = grad_values
                    keys_sum[:, lanes] = grad_keys
                else:
                    values_sum[0:stop, lanes] += grad_values
                    keys_sum[0:stop, lanes] += grad_keys
                halves.append(t_mm(keys, grad_scores))
            low = pair * 2 * HD
            out_ref[block * BLOCK : stop, low : low + 2 * HD] = (
                jnp.concatenate(halves, 0).T * scale
            ).astype(BF)
        out_ref[:, width + low : width + low + 2 * HD] = (keys_sum[...] * scale).astype(BF)
        out_ref[:, 2 * width + low : 2 * width + low + 2 * HD] = values_sum[...].astype(BF)


def rows_spec(width):
    return pl.BlockSpec((LEN, width), lambda i: (i, 0))


def attend(qkv):
    rows, width = qkv.shape[0], qkv.shape[1] // 3
    return pl.pallas_call(
        attend_kernel,
        grid=(rows // LEN,),
        in_specs=[rows_spec(3 * width)],
        out_specs=rows_spec(width),
        out_shape=jax.ShapeDtypeStruct((rows, width), BF),
        cost_estimate=pl.CostEstimate(
            flops=1_000_000_000, bytes_accessed=rows * width, transcendentals=0
        ),
        compiler_params=pltpu.CompilerParams(vmem_limit_bytes=48 * 1024 * 1024),
        name="attend",
    )(qkv)


def attend_back(qkv, grad):
    rows, width = grad.shape
    return pl.pallas_call(
        attend_back_kernel,
        grid=(rows // LEN,),
        in_specs=[rows_spec(3 * width), rows_spec(width)],
        out_specs=rows_spec(3 * width),
        out_shape=jax.ShapeDtypeStruct((rows, 3 * width), BF),
        scratch_shapes=[pltpu.VMEM((LEN, 2 * HD), F32), pltpu.VMEM((LEN, 2 * HD), F32)],
        cost_estimate=pl.CostEstimate(
            flops=1_000_000_000, bytes_accessed=rows * width, transcendentals=0
        ),
        compiler_params=pltpu.CompilerParams(vmem_limit_bytes=48 * 1024 * 1024),
        name="attend_back",
    )(qkv, grad)


def pack(flat):
    size = flat.shape[-1]
    full = -(-size // 1024) * 1024
    flat = jnp.pad(flat, [(0, 0)] * (flat.ndim - 1) + [(0, full - size)])
    return flat.reshape(flat.shape[:-1] + (full // 128, 128))


def on_device_wide(
    tokens,
    ln1_gain,
    ln1_bias,
    qkv_weight,
    qv_bias,
    out_weight,
    out_bias,
    ln2_gain,
    ln2_bias,
    fc_weight,
    fc_bias,
    proj_weight,
    proj_bias,
    out_grad,
):
    both = ("fsdp", "tensor")
    n_fsdp, n_tensor = lax.axis_size("fsdp"), lax.axis_size("tensor")
    me = lax.axis_index("tensor")
    part = ln1_gain.shape[0]
    width = out_weight.shape[0]
    heads = width // HD
    hidden = fc_weight.shape[1]
    model = tokens.shape[1]
    vectors = jnp.concatenate(
        [
            ln1_gain,
            ln1_bias,
            ln2_gain,
            ln2_bias,
            out_bias,
            proj_bias,
            qv_bias.astype(F32).reshape(-1),
            fc_bias.astype(F32).reshape(-1),
        ]
    )
    bundle = lax.all_gather(pack(vectors), both, axis=0, tiled=False)
    bundle = bundle.reshape(n_fsdp * n_tensor, -1)
    gain_one, bias_one, gain_two, bias_two, bias_out, bias_proj = (
        bundle[:, i * part : (i + 1) * part].reshape(-1) for i in range(6)
    )
    mine = lax.dynamic_index_in_dim(bundle.reshape(n_fsdp, n_tensor, -1), me, 1, keepdims=False)
    low, high = 6 * part, 6 * part + qv_bias.size
    qv_full = (
        mine[:, low:high].reshape((n_fsdp,) + qv_bias.shape).transpose(1, 2, 0, 3).reshape(2, width)
    )
    fcb_full = (
        mine[:, high : high + fc_bias.size]
        .reshape((n_fsdp,) + fc_bias.shape)
        .transpose(1, 0, 2)
        .reshape(hidden)
    )
    bias_row = jnp.concatenate([qv_full[0], jnp.zeros((width,), F32), qv_full[1]])
    joined = lax.all_gather(
        qkv_weight.reshape(qkv_weight.shape[0], 3 * width), "fsdp", axis=0, tiled=True
    )
    out_full = lax.all_gather(out_weight, "fsdp", axis=1, tiled=True)
    fc_full = lax.all_gather(fc_weight, "fsdp", axis=0, tiled=True)
    proj_full = lax.all_gather(proj_weight, "fsdp", axis=1, tiled=True)

    inputs = tokens.astype(F32)
    normed_one = gather_rows(layer_norm(inputs, gain_one, bias_one).astype(BF))
    qkv = in_order([(mm(piece, joined) + bias_row).astype(BF) for piece in normed_one])
    attended = attend(qkv)
    att = [take_rows(attended, k) for k in range(chunk_count())]
    grads = gather_rows(after(out_grad, qkv))
    middle = inputs + (sum_rows(lambda k: mm(att[k], out_full)) + bias_out)
    normed_two = gather_rows(layer_norm(middle, gain_two, bias_two).astype(BF))
    before = [mm(piece, fc_full) + fcb_full for piece in normed_two]
    act = [gelu_tanh(piece).astype(BF) for piece in before]

    grad_pre = []
    for piece, grad in zip(before, grads):
        pull = jax.vjp(gelu_tanh, piece)[1]
        grad_pre.append(pull(mm_t(grad, proj_full))[0].astype(BF))
    grad_normed_two = sum_rows(lambda k: mm_t(grad_pre[k], fc_full))
    grad_pre_all = joined_rows(grad_pre)
    grad_proj = t_mm(joined_rows(act), joined_rows(grads)).astype(BF)
    grad_fc = t_mm(joined_rows(normed_two), grad_pre_all).astype(BF)
    grad_fc_bias = jnp.sum(grad_pre_all, 0, dtype=F32)
    grad_proj_bias = jnp.sum(out_grad, 0, dtype=F32)
    norm_pull_two = jax.vjp(layer_norm, middle, gain_two, bias_two)[1]
    grad_middle_part, grad_gain_two, grad_bias_two = norm_pull_two(grad_normed_two)
    grad_middle = out_grad.astype(F32) + grad_middle_part
    grad_branch = grad_middle.astype(BF)
    grad_out_bias = jnp.sum(grad_branch, 0, dtype=F32)
    branches = gather_rows(grad_branch)
    grad_attended = in_order([mm_t(piece, out_full).astype(BF) for piece in branches])

    late = lax.optimization_barrier((grad_attended, *act))
    grad_attended, act = late[0], late[1:]
    output = middle + sum_rows(lambda k: mm(act[k], proj_full)) + bias_proj
    grad_qkv = attend_back(qkv, grad_attended)
    grad_out = t_mm(joined_rows(att), joined_rows(branches)).astype(BF)
    pieces = [take_rows(grad_qkv, k) for k in range(chunk_count())]
    grad_normed_one = sum_rows(lambda k: mm_t(pieces[k], joined))
    pieces_all = joined_rows(pieces)
    grad_joined = t_mm(joined_rows(normed_one), pieces_all).astype(BF)
    qkv_sums = jnp.sum(pieces_all, 0, dtype=F32)
    norm_pull_one = jax.vjp(layer_norm, inputs, gain_one, bias_one)[1]
    grad_input_part, grad_gain_one, grad_bias_one = norm_pull_one(grad_normed_one)
    input_grad = grad_middle + grad_input_part

    def scatter(value, dim):
        return replica_sum(
            lax.psum_scatter(value, "fsdp", scatter_dimension=dim, tiled=True).astype(BF)
        )

    total_proj = scatter(grad_proj, 1)
    total_fc = scatter(grad_fc, 0)
    total_out = scatter(grad_out, 1)
    total_joined = scatter(grad_joined, 0)

    wide = jnp.stack(
        [grad_gain_one, grad_bias_one, grad_gain_two, grad_bias_two, grad_out_bias, grad_proj_bias]
    )
    wide = wide.reshape(6, n_fsdp * n_tensor, part).transpose(1, 0, 2).reshape(-1, 6 * part)
    grad_qv = jnp.stack([qkv_sums[:width], qkv_sums[2 * width :]])
    grad_qv = grad_qv.reshape(2, heads, n_fsdp, -1).transpose(2, 0, 1, 3).reshape(n_fsdp, -1)
    grad_fcb = grad_fc_bias.reshape(fc_bias.shape[0], n_fsdp, -1).transpose(1, 0, 2)
    own = jnp.concatenate([grad_qv, grad_fcb.reshape(n_fsdp, -1)], -1)
    is_me = (jnp.arange(n_tensor, dtype=jnp.int32) == me)[None, :, None]
    own = jnp.where(is_me, own[:, None, :], 0.0).reshape(n_fsdp * n_tensor, -1)
    sums = lax.psum_scatter(
        pack(jnp.concatenate([wide, own], -1)), both, scatter_dimension=0, tiled=False
    )
    sums = replica_sum(sums).reshape(-1)
    vec = [sums[i * part : (i + 1) * part] for i in range(6)]
    total_qv = sums[low:high].reshape(qv_bias.shape)
    total_fcb = sums[high : high + fc_bias.size].reshape(fc_bias.shape)
    return (
        output,
        input_grad,
        vec[0],
        vec[1],
        total_joined.reshape(qkv_weight.shape),
        total_qv,
        total_out,
        vec[4],
        vec[2],
        vec[3],
        total_fc,
        total_fcb,
        total_proj,
        vec[5],
    )


MESH = pl.DeviceIdType.MESH
HALF = LEN // 2


def chip_swap(value):
    return swap(value, 2)


def y_swap(value):
    return lax.ppermute(value, "replica", [(0, 1), (1, 0)])


def put(full, piece, row, column=0):
    return lax.dynamic_update_slice(full, piece, (row, jnp.int32(column)))


def rows_at(full, row, count):
    return lax.dynamic_slice_in_dim(full, row, count, 0)


def two(first, second, index, dim=0):
    low = jnp.concatenate([first, second], dim)
    high = jnp.concatenate([second, first], dim)
    return jnp.where(index == 0, low, high)


def half_of(value, index, dim):
    low, high = jnp.split(value, 2, dim)
    return jnp.where(index == 0, low, high)


def y_send(value, dim):
    y = lax.axis_index("replica")
    return half_of(value, y, dim), y_swap(half_of(value, 1 - y, dim))


def plus(left, right):
    return (left.astype(F32) + right.astype(F32)).astype(BF)


def group_peer(step):
    n_fsdp, n_tensor = lax.axis_size("fsdp"), lax.axis_size("tensor")
    size = n_fsdp * n_tensor
    me = lax.axis_index("fsdp") * n_tensor + lax.axis_index("tensor")
    peer = lax.rem(me + step, size)
    place = (lax.axis_index("replica"), peer // n_tensor, lax.rem(peer, n_tensor))
    return me, peer, place


def greet(size):
    barrier = pltpu.get_barrier_semaphore()
    for step in range(1, size):
        pl.semaphore_signal(
            barrier, inc=1, device_id=group_peer(step)[2], device_id_type=MESH
        )
    pl.semaphore_wait(barrier, size - 1)


def opening_kernel(
    vec_ref,
    shard_ref,
    fc_ref,
    bundle_ref,
    full_ref,
    fc_all_ref,
    vsend,
    vrecv,
    zsend,
    zrecv,
    xsend,
    xrecv,
    ysend,
    yrecv,
    fsend,
    frecv,
):
    size, count = bundle_ref.shape[0], full_ref.shape[1]
    r, f, t = (lax.axis_index(name) for name in ("replica", "fsdp", "tensor"))
    x_place = (r, f, lax.rem(t + 2, 4))
    y_place = (1 - r, f, t)
    barrier = pltpu.get_barrier_semaphore()
    for step in range(1, size):
        pl.semaphore_signal(
            barrier, inc=1, device_id=group_peer(step)[2], device_id_type=MESH
        )
    pl.semaphore_signal(barrier, inc=1, device_id=y_place, device_id_type=MESH)
    pl.semaphore_wait(barrier, size)

    def send(src, dst, send_sem, recv_sem, place):
        copy = pltpu.make_async_remote_copy(
            src_ref=src,
            dst_ref=dst,
            send_sem=send_sem,
            recv_sem=recv_sem,
            device_id=place,
            device_id_type=MESH,
        )
        copy.start()
        return copy

    along_z = []
    for k in range(1, count):
        place = (r, lax.rem(f + k, count), t)
        along_z.append(
            send(shard_ref.at[r], full_ref.at[0, f, r], zsend.at[k], zrecv.at[k], place)
        )
    rest = []
    for h in range(2):
        rest.append(
            send(shard_ref.at[h], full_ref.at[1, f, h], xsend.at[h], xrecv.at[h], x_place)
        )
    for step in range(1, size):
        me, _, place = group_peer(step)
        rest.append(send(vec_ref, bundle_ref.at[me], vsend.at[step], vrecv.at[step], place))
    for k in range(1, count):
        place = (r, lax.rem(f + k, count), t)
        rest.append(send(fc_ref, fc_all_ref.at[f], fsend.at[k], frecv.at[k], place))
    bundle_ref[group_peer(0)[0]] = vec_ref[...]
    full_ref[0, f] = shard_ref[...]
    fc_all_ref[f] = fc_ref[...]
    along_x = []
    for k in range(1, count):
        along_z[k - 1].wait_recv()
        come = lax.rem(f + count - k, count)
        block = full_ref.at[0, come, r]
        along_x.append(
            send(block, full_ref.at[1, come, r], xsend.at[1 + k], xrecv.at[1 + k], x_place)
        )
        rest.append(send(block, block, ysend.at[k - 1], yrecv.at[k - 1], y_place))
    for k in range(1, count):
        along_x[k - 1].wait_recv()
        come = lax.rem(f + count - k, count)
        block = full_ref.at[1, come, r]
        slot = count + k - 2
        rest.append(send(block, block, ysend.at[slot], yrecv.at[slot], y_place))
    for copy in along_z + along_x:
        copy.wait_send()
    for copy in rest:
        copy.wait()


def small_scatter_kernel(in_ref, out_ref, held, send, recv):
    size = in_ref.shape[0]
    greet(size)
    copies = []
    for step in range(1, size):
        _, peer, place = group_peer(step)
        copy = pltpu.make_async_remote_copy(
            src_ref=in_ref.at[peer],
            dst_ref=held.at[step],
            send_sem=send.at[step],
            recv_sem=recv.at[step],
            device_id=place,
            device_id_type=MESH,
        )
        copy.start()
        copies.append(copy)
    total = in_ref[group_peer(0)[0]]
    for step, copy in enumerate(copies):
        copy.wait()
        total = total + held[step + 1]
    out_ref[...] = total


def opening(vectors, shard, fc_shard, n_fsdp, n_tensor):
    size = n_fsdp * n_tensor
    halves = shard.reshape(2, shard.shape[0] // 2, shard.shape[1])
    whole = pl.BlockSpec(memory_space=pltpu.VMEM)
    dma = pltpu.SemaphoreType.DMA
    return pl.pallas_call(
        opening_kernel,
        in_specs=[whole, whole, whole],
        out_specs=[whole, whole, whole],
        out_shape=[
            jax.ShapeDtypeStruct((size,) + vectors.shape, F32),
            jax.ShapeDtypeStruct((2, n_fsdp) + halves.shape, BF),
            jax.ShapeDtypeStruct((n_fsdp,) + fc_shard.shape, BF),
        ],
        scratch_shapes=[dma((size,)), dma((size,)), dma((n_fsdp,)), dma((n_fsdp,))]
        + [dma((n_fsdp + 1,)), dma((n_fsdp + 1,)), dma((2 * n_fsdp,)), dma((2 * n_fsdp,))]
        + [dma((n_fsdp,)), dma((n_fsdp,))],
        compiler_params=pltpu.CompilerParams(
            collective_id=1, has_side_effects=True, vmem_limit_bytes=32 * 1024 * 1024
        ),
        name="opening",
    )(vectors, halves, fc_shard)


def small_scatter(value):
    size = value.shape[0]
    return pl.pallas_call(
        small_scatter_kernel,
        in_specs=[pl.BlockSpec(memory_space=pltpu.VMEM)],
        out_specs=pl.BlockSpec(memory_space=pltpu.VMEM),
        out_shape=jax.ShapeDtypeStruct(value.shape[1:], F32),
        scratch_shapes=[
            pltpu.VMEM(value.shape, F32),
            pltpu.SemaphoreType.DMA((size,)),
            pltpu.SemaphoreType.DMA((size,)),
        ],
        compiler_params=pltpu.CompilerParams(collective_id=2, has_side_effects=True),
        name="small_scatter",
    )(value)


def attend_own_kernel(qkv_ref, out_ref):
    start = pl.multiple_of((lax.axis_index("tensor") // 2) * HALF, HALF)
    attend_kernel(qkv_ref.at[pl.ds(start, LEN)], out_ref)


def attend_back_own_kernel(qkv_ref, grad_ref, out_ref, keys_sum, values_sum):
    start = pl.multiple_of((lax.axis_index("tensor") // 2) * HALF, HALF)
    rows = pl.ds(start, LEN)
    attend_back_kernel(qkv_ref.at[rows], grad_ref.at[rows], out_ref, keys_sum, values_sum)


def attend_own(qkv):
    rows, width = qkv.shape[0], qkv.shape[1] // 6
    return pl.pallas_call(
        attend_own_kernel,
        grid=(2,),
        in_specs=[pl.BlockSpec((rows, 3 * width), lambda i: (0, i))],
        out_specs=pl.BlockSpec((LEN, width), lambda i: (0, i)),
        out_shape=jax.ShapeDtypeStruct((LEN, 2 * width), BF),
        cost_estimate=pl.CostEstimate(
            flops=1_000_000_000, bytes_accessed=LEN * width, transcendentals=0
        ),
        compiler_params=pltpu.CompilerParams(vmem_limit_bytes=48 * 1024 * 1024),
        name="attend_own",
    )(qkv)


def attend_back_own(qkv, grad, group):
    rows, width = qkv.shape[0], qkv.shape[1] // 6
    return pl.pallas_call(
        attend_back_own_kernel,
        grid=(1,),
        in_specs=[
            pl.BlockSpec((rows, 3 * width), lambda i: (0, group)),
            pl.BlockSpec((rows, width), lambda i: (0, group)),
        ],
        out_specs=pl.BlockSpec((LEN, 3 * width), lambda i: (0, 0)),
        out_shape=jax.ShapeDtypeStruct((LEN, 3 * width), BF),
        scratch_shapes=[pltpu.VMEM((LEN, 2 * HD), F32), pltpu.VMEM((LEN, 2 * HD), F32)],
        cost_estimate=pl.CostEstimate(
            flops=1_000_000_000, bytes_accessed=LEN * width, transcendentals=0
        ),
        compiler_params=pltpu.CompilerParams(vmem_limit_bytes=48 * 1024 * 1024),
        name="attend_back_own",
    )(qkv, grad)


ROOT = (2.0 / 3.141592653589793) ** 0.5


def hidden_kernel(own_ref, side_ref, weight_ref, bias_ref, act_ref, slope_ref):
    rows = own_ref.shape[0]
    for k, ref in enumerate((own_ref, side_ref)):
        for low in range(0, rows, BLOCK):
            pre = mm(ref[low : low + BLOCK], weight_ref[...]) + bias_ref[...]
            square = pre * pre
            bent = jnp.tanh(ROOT * pre * (1.0 + 0.044715 * square))
            half = 0.5 * (1.0 + bent)
            place = slice(k * rows + low, k * rows + low + BLOCK)
            act_ref[place] = (pre * half).astype(BF)
            rise = ROOT * (1.0 + 3 * 0.044715 * square)
            slope = half + 0.5 * pre * (1.0 - bent * bent) * rise
            slope_ref[place] = slope.astype(BF)


def hidden_layer(own, side, weight, bias):
    rows, model = own.shape
    hidden = weight.shape[1]
    size = 256
    whole = pl.BlockSpec((rows, model), lambda i: (0, 0))
    result = pl.BlockSpec((2 * rows, size), lambda i: (0, i))
    return pl.pallas_call(
        hidden_kernel,
        grid=(hidden // size,),
        in_specs=[
            whole,
            whole,
            pl.BlockSpec((model, size), lambda i: (0, i)),
            pl.BlockSpec((1, size), lambda i: (0, i)),
        ],
        out_specs=[result, result],
        out_shape=[jax.ShapeDtypeStruct((2 * rows, hidden), BF)] * 2,
        cost_estimate=pl.CostEstimate(
            flops=1_000_000_000, bytes_accessed=LEN * 256, transcendentals=0
        ),
        compiler_params=pltpu.CompilerParams(vmem_limit_bytes=48 * 1024 * 1024),
        name="hidden_layer",
    )(own, side, weight, bias.reshape(1, hidden))


def hidden_back_kernel(
    grad_ref, proj_ref, slope_ref, weight_ref, pre_ref, sum_ref, own_ref, side_ref, total
):
    step = pl.program_id(0)
    rows = own_ref.shape[0]
    size = proj_ref.shape[0]
    sums = jnp.zeros((1, size), F32)
    for low in range(0, 2 * rows, 3 * BLOCK):
        place = slice(low, low + 3 * BLOCK)
        grad = mm_t(grad_ref[place], proj_ref[...]) * slope_ref[place].astype(F32)
        grad = grad.astype(BF)
        pre_ref[place] = grad
        sums = sums + jnp.sum(grad.astype(F32), 0, keepdims=True)
        part = mm_t(grad, weight_ref[...])

        @pl.when(step == 0)
        def _():
            total[place] = part

        @pl.when(step > 0)
        def _():
            total[place] += part

    sum_ref[...] = sums

    @pl.when(step == pl.num_programs(0) - 1)
    def _():
        own_ref[...] = total[:rows]
        side_ref[...] = total[rows:].astype(BF)


def hidden_back(grads, proj, slope, weight):
    full, model = grads.shape
    hidden = proj.shape[0]
    size = 512
    block = pl.BlockSpec((full, size), lambda i: (0, i))
    half = pl.BlockSpec((full // 2, model), lambda i: (0, 0))
    return pl.pallas_call(
        hidden_back_kernel,
        grid=(hidden // size,),
        in_specs=[
            pl.BlockSpec((full, model), lambda i: (0, 0)),
            pl.BlockSpec((size, model), lambda i: (i, 0)),
            block,
            pl.BlockSpec((model, size), lambda i: (0, i)),
        ],
        out_specs=[block, pl.BlockSpec((1, size), lambda i: (0, i)), half, half],
        out_shape=[
            jax.ShapeDtypeStruct((full, hidden), BF),
            jax.ShapeDtypeStruct((1, hidden), F32),
            jax.ShapeDtypeStruct((full // 2, model), F32),
            jax.ShapeDtypeStruct((full // 2, model), BF),
        ],
        scratch_shapes=[pltpu.VMEM((full, model), F32)],
        cost_estimate=pl.CostEstimate(
            flops=1_000_000_000, bytes_accessed=LEN * 256, transcendentals=0
        ),
        compiler_params=pltpu.CompilerParams(vmem_limit_bytes=52 * 1024 * 1024),
        name="hidden_back",
    )(grads, proj, slope, weight)


def z_scatter(value, dim):
    count = lax.axis_size("fsdp")
    f = lax.axis_index("fsdp")
    size = value.shape[dim] // count

    def piece(k):
        place = lax.rem(f + k, count) * size
        return lax.dynamic_slice_in_dim(value, place, size, dim)

    total = piece(0).astype(F32)
    for k in range(1, count):
        pairs = [(i, (i + k) % count) for i in range(count)]
        total = total + lax.ppermute(piece(k), "fsdp", pairs).astype(F32)
    return total.astype(BF)


def on_device_chip(
    tokens,
    ln1_gain,
    ln1_bias,
    qkv_weight,
    qv_bias,
    out_weight,
    out_bias,
    ln2_gain,
    ln2_bias,
    fc_weight,
    fc_bias,
    proj_weight,
    proj_bias,
    out_grad,
):
    n_fsdp, n_tensor = lax.axis_size("fsdp"), lax.axis_size("tensor")
    group = n_fsdp * n_tensor
    me = lax.axis_index("tensor")
    x, core = me // 2, me % 2
    y = lax.axis_index("replica")
    part = ln1_gain.shape[0]
    width = out_weight.shape[0]
    heads = width // HD
    hidden = fc_weight.shape[1]
    rows, model = tokens.shape
    mid_row = (1 - x) * LEN
    own_row = x * HALF
    row_of = (core * rows, (1 - core) * rows)

    vectors = jnp.concatenate(
        [
            ln1_gain,
            ln1_bias,
            ln2_gain,
            ln2_bias,
            out_bias,
            proj_bias,
            qv_bias.astype(F32).reshape(-1),
            fc_bias.astype(F32).reshape(-1),
        ]
    )
    flat_qkv = qkv_weight.reshape(qkv_weight.shape[0], 3 * width)
    fc_half = half_of(fc_weight, y, 1)
    bundle, joined, fc_mine = opening(pack(vectors), flat_qkv, fc_half, n_fsdp, n_tensor)
    fc_mine = fc_mine.reshape(model, hidden // 2)
    bundle, joined = bundle.reshape(group, -1), joined.reshape(2, model, 3 * width)
    gain_one, bias_one, gain_two, bias_two, bias_out, bias_proj = (
        bundle[:, i * part : (i + 1) * part].reshape(-1) for i in range(6)
    )
    by_tensor = bundle.reshape(n_fsdp, n_tensor, -1)
    low, high = 6 * part, 6 * part + qv_bias.size
    bias_rows, fcb_rows = [], []
    for place in (me, me ^ 2):
        mine = lax.dynamic_index_in_dim(by_tensor, place, 1, keepdims=False)
        qv = (
            mine[:, low:high]
            .reshape((n_fsdp,) + qv_bias.shape)
            .transpose(1, 2, 0, 3)
            .reshape(2, width)
        )
        bias_rows.append(jnp.concatenate([qv[0], jnp.zeros((width,), F32), qv[1]]))
        fcb = (
            mine[:, high : high + fc_bias.size]
            .reshape((n_fsdp,) + fc_bias.shape)
            .transpose(1, 0, 2)
            .reshape(hidden)
        )
        fcb_rows += [half_of(fcb, y, 0), half_of(fcb, 1 - y, 0)]
    fcb_full = jnp.concatenate(fcb_rows)

    proj_and_out = jnp.concatenate([half_of(proj_weight, y, 0), out_weight], 0)
    proj_and_out = lax.all_gather(after(proj_and_out, fc_mine), "fsdp", axis=1, tiled=True)
    proj_mine, out_near = proj_and_out[: hidden // 2], proj_and_out[hidden // 2 :]
    fc_far, fc_back = chip_swap(fc_mine), y_swap(fc_mine)
    fc_last = y_swap(fc_far)
    fc_full = jnp.concatenate([fc_mine, fc_back, fc_far, fc_last], 1)
    out_far = chip_swap(out_near)
    out_full = jnp.concatenate([out_near, out_far], 0)
    proj_far, proj_back = chip_swap(proj_mine), y_swap(proj_mine)
    proj_last = y_swap(proj_far)

    def pair(local):
        return [local, swap(local, 1)]

    def pair_sum(term):
        side = swap(term(1).astype(BF), 1)
        return term(0) + side.astype(F32)

    inputs = tokens.astype(F32)
    normed_one = pair(layer_norm(inputs, gain_one, bias_one).astype(BF))
    qkv = jnp.zeros((2 * rows, 6 * width), BF)
    for j in range(2):
        for k in range(2):
            piece = (mm(normed_one[k], joined[j]) + bias_rows[j]).astype(BF)
            qkv = put(qkv, piece, row_of[k], 3 * width * j)
    qkv_mid_half = rows_at(qkv, mid_row, HALF)
    mid_far = chip_swap(after(qkv_mid_half[:, 3 * width :], fc_far))
    att_own = attend_own(after(qkv, fc_back, fc_far))
    qkv_mid = two(qkv_mid_half[:, : 3 * width], mid_far, x)
    att_mid = attend(after(qkv_mid, fc_last))
    att_far = chip_swap(rows_at(att_mid, (1 - x) * HALF, HALF))
    attended = jnp.zeros((2 * rows, 2 * width), BF)
    attended = put(attended, att_own, own_row)
    attended = put(attended, rows_at(att_mid, x * HALF, HALF), mid_row)
    attended = put(attended, after(att_far, proj_mine), mid_row, width)
    att = [rows_at(attended, row_of[k], rows) for k in range(2)]
    grads = pair(after(out_grad, qkv))
    middle = inputs + (pair_sum(lambda k: mm(att[k], out_full)) + bias_out)
    middle = after(middle, proj_far, proj_back)
    normed_two = pair(layer_norm(middle, gain_two, bias_two).astype(BF))
    act_all, slope = hidden_layer(normed_two[0], normed_two[1], fc_full, fcb_full)
    grads_all = joined_rows(grads)
    grad_proj = t_mm(act_all, grads_all).astype(BF)
    grad_proj = grad_proj.reshape(2, 2, hidden // 2, model)
    proj_keep, proj_come = grad_proj[:, 0], y_swap(grad_proj[:, 1])
    proj_full = after(proj_mine, grad_proj), after(proj_back, grad_proj)
    proj_full += after(proj_far, grad_proj), after(proj_last, grad_proj)
    proj_full = jnp.concatenate(proj_full, 0)
    grad_pre_all, grad_fc_bias, back_here, back_side = hidden_back(
        after(grads_all, grad_proj), proj_full, slope, fc_full
    )
    grad_fc_bias = grad_fc_bias.reshape(-1)
    grad_normed_two = back_here + swap(back_side, 1).astype(F32)
    act = [act_all[:rows], act_all[rows:]]
    grad_proj_bias = jnp.sum(out_grad, 0, dtype=F32)
    norm_pull_two = jax.vjp(layer_norm, middle, gain_two, bias_two)[1]
    grad_middle_part, grad_gain_two, grad_bias_two = norm_pull_two(grad_normed_two)
    grad_middle = out_grad.astype(F32) + grad_middle_part
    grad_branch = grad_middle.astype(BF)
    grad_out_bias = jnp.sum(grad_branch, 0, dtype=F32)
    branches = pair(grad_branch)
    grad_fc = t_mm(joined_rows(normed_two), after(grad_pre_all, grad_branch)).astype(BF)
    cols = hidden // 2
    fc_keep = jnp.stack([grad_fc[:, :cols], grad_fc[:, 2 * cols : 3 * cols]])
    fc_sent = jnp.stack([grad_fc[:, cols : 2 * cols], grad_fc[:, 3 * cols :]])
    fc_come = y_swap(fc_sent)
    grad_attended = jnp.zeros((2 * rows, 2 * width), BF)
    for k in range(2):
        grad_attended = put(grad_attended, mm_t(branches[k], out_full).astype(BF), row_of[k])

    grad_mid_half = rows_at(grad_attended, mid_row, HALF)
    grad_mid_far = chip_swap(grad_mid_half[:, width:])
    late = lax.optimization_barrier((grad_attended, *act))
    grad_attended, act = late[0], late[1:]
    output = middle + pair_sum(lambda k: mm(act[k], proj_full)) + bias_proj
    grad_mid = two(grad_mid_half[:, :width], grad_mid_far, x)
    back_mid = attend_back(qkv_mid, after(grad_mid, output, fc_sent))
    back_far = chip_swap(rows_at(back_mid, (1 - x) * HALF, HALF))
    proj_sum = plus(proj_keep, after(proj_come, back_mid))
    proj_over = chip_swap(after(proj_sum[1], grad_mid_far))
    cut = 3 * width
    normed_all = joined_rows(normed_one)

    def grads_of(kept, middle_part, own_part):
        full = jnp.zeros((2 * rows, cut), BF)
        full = put(put(full, own_part, own_row), middle_part, mid_row)
        pieces = [rows_at(full, row_of[k], rows) for k in range(2)]
        every = joined_rows(pieces)
        return pieces, jnp.sum(every, 0, dtype=F32), t_mm(normed_all, every).astype(BF)

    own_far = attend_back_own(qkv, after(grad_attended, back_mid, proj_sum), 1)
    far_rows, far_totals, joined_far = grads_of(1, after(back_far, own_far), own_far)
    far_keep, far_come = y_send(joined_far, 1)
    proj_part = plus(proj_sum[0], after(proj_over, own_far))
    proj_own = lax.psum_scatter(proj_part, "fsdp", scatter_dimension=1, tiled=True).astype(BF)
    own_near = attend_back_own(qkv, after(grad_attended, joined_far, proj_part), 0)
    grad_out = t_mm(joined_rows(att), after(joined_rows(branches), joined_far)).astype(BF)
    out_keep, out_come = y_send(grad_out.reshape(2, width, model), 1)
    fc_sum = plus(fc_keep, after(fc_come, own_far))
    fc_over = chip_swap(fc_sum[1])
    fc_part = plus(fc_sum[0], after(fc_over, own_near))
    near_rows, near_totals, joined_close = grads_of(
        0, rows_at(back_mid, x * HALF, HALF), after(own_near, fc_part, far_come)
    )
    near_keep, near_come = y_send(joined_close, 1)
    far_sum = plus(far_keep, after(far_come, joined_close))
    qkv_over = chip_swap(far_sum)
    qkv_sums = jnp.concatenate([near_totals, far_totals])
    gated = [
        jnp.concatenate([near_rows[k], after(far_rows[k], far_sum)], 1) for k in range(2)
    ]
    joined_both = jnp.concatenate([joined[0], joined[1]], 1)
    out_sum = plus(out_keep, after(out_come, joined_close))
    out_over = chip_swap(out_sum[1])
    grad_normed_one = pair_sum(lambda k: mm_t(gated[k], joined_both))
    fc_own = lax.psum_scatter(fc_part, "fsdp", scatter_dimension=0, tiled=True).astype(BF)
    out_part = plus(out_sum[0], after(out_over, grad_normed_one))
    out_own = lax.psum_scatter(out_part, "fsdp", scatter_dimension=1, tiled=True).astype(BF)
    norm_pull_one = jax.vjp(layer_norm, inputs, gain_one, bias_one)[1]
    grad_input_part, grad_gain_one, grad_bias_one = norm_pull_one(grad_normed_one)
    input_grad = grad_middle + grad_input_part
    near_come = after(near_come, grad_normed_one)
    near_sum = near_keep.astype(F32) + near_come.astype(F32)
    qkv_part = plus(near_sum, after(qkv_over, grad_normed_one))
    qkv_own = z_scatter(qkv_part, 0)

    def whole(mine, dim):
        return two(mine, y_swap(mine), y, dim).astype(F32)

    total_proj = whole(proj_own, 0)
    total_fc = whole(fc_own, 1)
    total_out = whole(out_own, 0)
    total_joined = whole(qkv_own, 1)

    wide = jnp.stack(
        [grad_gain_one, grad_bias_one, grad_gain_two, grad_bias_two, grad_out_bias, grad_proj_bias]
    )
    wide = wide.reshape(6, group, part).transpose(1, 0, 2).reshape(-1, 6 * part)
    own = []
    for j in range(2):
        sums = qkv_sums[j * cut : (j + 1) * cut]
        grad_qv = jnp.stack([sums[:width], sums[2 * width :]])
        grad_qv = grad_qv.reshape(2, heads, n_fsdp, -1).transpose(2, 0, 1, 3).reshape(n_fsdp, -1)
        first, second = jnp.split(grad_fc_bias[j * hidden : (j + 1) * hidden], 2)
        grad_fcb = two(first, second, y)
        grad_fcb = grad_fcb.reshape(fc_bias.shape[0], n_fsdp, -1).transpose(1, 0, 2)
        own.append(jnp.concatenate([grad_qv, grad_fcb.reshape(n_fsdp, -1)], -1))
    index = jnp.arange(n_tensor, dtype=jnp.int32)[None, :, None]
    own = jnp.where(
        index == me, own[0][:, None, :], jnp.where(index == (me ^ 2), own[1][:, None, :], 0.0)
    ).reshape(group, -1)
    sums = replica_sum(small_scatter(pack(jnp.concatenate([wide, own], -1)))).reshape(-1)
    vec = [sums[i * part : (i + 1) * part] for i in range(6)]
    total_qv = sums[low:high].reshape(qv_bias.shape)
    total_fcb = sums[high : high + fc_bias.size].reshape(fc_bias.shape)
    return (
        output,
        input_grad,
        vec[0],
        vec[1],
        total_joined.reshape(qkv_weight.shape),
        total_qv,
        total_out,
        vec[4],
        vec[2],
        vec[3],
        total_fc,
        total_fcb,
        total_proj,
        vec[5],
    )


def on_device(*arrays):
    pairs = lax.axis_size("tensor") == 4 and lax.axis_size("replica") == 2
    if pairs and 2 * arrays[0].shape[0] == LEN + HALF:
        return on_device_chip(*arrays)
    return on_device_wide(*arrays)


def solution(mesh):
    placed = (
        P(("replica", "fsdp", "tensor"), None),
        P(("fsdp", "tensor")),
        P(("fsdp", "tensor")),
        P("fsdp", None, "tensor"),
        P(None, "tensor", "fsdp"),
        P("tensor", "fsdp"),
        P(("fsdp", "tensor")),
        P(("fsdp", "tensor")),
        P(("fsdp", "tensor")),
        P("fsdp", "tensor"),
        P("tensor", "fsdp"),
        P("tensor", "fsdp"),
        P(("fsdp", "tensor")),
        P(("replica", "fsdp", "tensor"), None),
    )
    return jax.shard_map(
        on_device,
        mesh=mesh,
        in_specs=placed,
        out_specs=(
            P(("replica", "fsdp", "tensor"), None),
            P(("replica", "fsdp", "tensor"), None),
            P(("fsdp", "tensor")),
            P(("fsdp", "tensor")),
            P("fsdp", None, "tensor"),
            P(None, "tensor", "fsdp"),
            P("tensor", "fsdp"),
            P(("fsdp", "tensor")),
            P(("fsdp", "tensor")),
            P(("fsdp", "tensor")),
            P("fsdp", "tensor"),
            P("tensor", "fsdp"),
            P("tensor", "fsdp"),
            P(("fsdp", "tensor")),
        ),
        check_vma=False,
    )
```

```python
import jax
import jax.numpy as jnp
from jax import lax
from jax.experimental import pallas as pl
from jax.experimental.pallas import tpu as pltpu
from jax.sharding import PartitionSpec as P

HD = 64
LEN = 1024


EPS = 1e-05
NEG = -1e30
BLOCK = 256
BF = jnp.bfloat16
F32 = jnp.float32


def dot(left, right, dims):
    return lax.dot_general(left, right, (dims, ((), ())), preferred_element_type=F32)


def mm(left, right):
    return dot(left, right, ((1,), (0,)))


def mm_t(left, right):
    return dot(left, right, ((1,), (1,)))


def t_mm(left, right):
    return dot(left, right, ((0,), (0,)))


def layer_norm(values, gain, bias):
    center = values - jnp.mean(values, -1, keepdims=True)
    spread = jnp.mean(center * center, -1, keepdims=True)
    return center * lax.rsqrt(spread + EPS) * gain + bias


def gelu_tanh(values):
    return jax.nn.gelu(values, approximate=True)


def swap(value, bit):
    size = lax.axis_size("tensor")
    return lax.ppermute(value, "tensor", [(i, i ^ bit) for i in range(size)])


def after(value, *others):
    return lax.optimization_barrier((value,) + others)[0]


def chunk_count():
    size = lax.axis_size("tensor")
    return 4 if size == 4 else 1


def gather_rows(local):
    if chunk_count() == 1:
        return [lax.all_gather(local, "tensor", axis=0, tiled=True)]
    sib = swap(local, 1)
    far = swap(local, 2)
    return [local, sib, far, swap(far, 1)]


def sum_rows(part):
    if chunk_count() == 1:
        return lax.psum_scatter(part(0), "tensor", scatter_dimension=0, tiled=True)
    side = swap(part(3).astype(BF), 1)
    cross = swap((part(2) + side.astype(F32)).astype(BF), 2)
    near = swap(part(1).astype(BF), 1)
    return part(0) + near.astype(F32) + cross.astype(F32)


def take_rows(full, k):
    if chunk_count() == 1:
        return full
    rows = full.shape[0] // 4
    return lax.dynamic_slice_in_dim(full, (lax.axis_index("tensor") ^ k) * rows, rows, 0)


def in_order(pieces):
    if len(pieces) == 1:
        return pieces[0]
    rows = pieces[0].shape[0]
    me = lax.axis_index("tensor")
    full = jnp.zeros((4 * rows, pieces[0].shape[1]), pieces[0].dtype)
    for k, piece in enumerate(pieces):
        full = lax.dynamic_update_slice_in_dim(full, piece, (me ^ k) * rows, 0)
    return full


def joined_rows(pieces):
    return pieces[0] if len(pieces) == 1 else jnp.concatenate(pieces, 0)


def replica_sum(value):
    size = lax.axis_size("replica")
    if size == 2:
        return value.astype(F32) + lax.ppermute(value, "replica", [(0, 1), (1, 0)]).astype(F32)
    return lax.psum(value, "replica").astype(F32)


def scores_t(qkv_ref, width, head, block):
    stop = (block + 1) * BLOCK
    low = head * HD
    query = qkv_ref[block * BLOCK : stop, low : low + HD]
    keys = qkv_ref[0:stop, width + low : width + low + HD]
    scores = mm_t(keys, query * jnp.asarray(HD ** (-0.5), BF))
    shape = (BLOCK, BLOCK)
    keep = lax.broadcasted_iota(jnp.int32, shape, 0) <= lax.broadcasted_iota(jnp.int32, shape, 1)
    edge = jnp.where(keep, scores[stop - BLOCK :], NEG)
    scores = edge if block == 0 else jnp.concatenate([scores[: stop - BLOCK], edge], 0)
    expo = jnp.exp(scores - jnp.max(scores, 0, keepdims=True))
    return query, keys, expo, 1.0 / jnp.sum(expo, 0, keepdims=True)


def attend_kernel(qkv_ref, out_ref):
    width = out_ref.shape[1]
    for pair in range(width // (2 * HD)):
        for block in range(LEN // BLOCK):
            stop = (block + 1) * BLOCK
            halves = []
            for head in (2 * pair, 2 * pair + 1):
                _, _, expo, inverse = scores_t(qkv_ref, width, head, block)
                low = 2 * width + head * HD
                values = qkv_ref[0:stop, low : low + HD]
                halves.append(t_mm(values, expo.astype(BF)) * inverse)
            out_ref[block * BLOCK : stop, pair * 2 * HD : (pair + 1) * 2 * HD] = (
                jnp.concatenate(halves, 0).T.astype(BF)
            )


def attend_back_kernel(qkv_ref, grad_ref, out_ref, keys_sum, values_sum):
    width = grad_ref.shape[1]
    scale = HD ** (-0.5)
    for pair in range(width // (2 * HD)):
        for block in reversed(range(LEN // BLOCK)):
            stop = (block + 1) * BLOCK
            halves = []
            for side in (0, 1):
                head = 2 * pair + side
                query, keys, expo, inverse = scores_t(qkv_ref, width, head, block)
                low = head * HD
                values = qkv_ref[0:stop, 2 * width + low : 2 * width + low + HD]
                grad = grad_ref[block * BLOCK : stop, low : low + HD]
                probs = expo * inverse
                grad_values = mm(probs.astype(BF), grad)
                grad_probs = mm_t(values, grad)
                weighted = probs * grad_probs
                total = jnp.sum(weighted, 0, keepdims=True)
                grad_scores = (weighted - probs * total).astype(BF)
                grad_keys = mm(grad_scores, query)
                lanes = slice(side * HD, (side + 1) * HD)
                if stop == LEN:
                    values_sum[:, lanes] = grad_values
                    keys_sum[:, lanes] = grad_keys
                else:
                    values_sum[0:stop, lanes] += grad_values
                    keys_sum[0:stop, lanes] += grad_keys
                halves.append(t_mm(keys, grad_scores))
            low = pair * 2 * HD
            out_ref[block * BLOCK : stop, low : low + 2 * HD] = (
                jnp.concatenate(halves, 0).T * scale
            ).astype(BF)
        out_ref[:, width + low : width + low + 2 * HD] = (keys_sum[...] * scale).astype(BF)
        out_ref[:, 2 * width + low : 2 * width + low + 2 * HD] = values_sum[...].astype(BF)


def rows_spec(width):
    return pl.BlockSpec((LEN, width), lambda i: (i, 0))


def attend(qkv):
    rows, width = qkv.shape[0], qkv.shape[1] // 3
    return pl.pallas_call(
        attend_kernel,
        grid=(rows // LEN,),
        in_specs=[rows_spec(3 * width)],
        out_specs=rows_spec(width),
        out_shape=jax.ShapeDtypeStruct((rows, width), BF),
        cost_estimate=pl.CostEstimate(
            flops=1_000_000_000, bytes_accessed=rows * width, transcendentals=0
        ),
        compiler_params=pltpu.CompilerParams(vmem_limit_bytes=48 * 1024 * 1024),
        name="attend",
    )(qkv)


def attend_back(qkv, grad):
    rows, width = grad.shape
    return pl.pallas_call(
        attend_back_kernel,
        grid=(rows // LEN,),
        in_specs=[rows_spec(3 * width), rows_spec(width)],
        out_specs=rows_spec(3 * width),
        out_shape=jax.ShapeDtypeStruct((rows, 3 * width), BF),
        scratch_shapes=[pltpu.VMEM((LEN, 2 * HD), F32), pltpu.VMEM((LEN, 2 * HD), F32)],
        cost_estimate=pl.CostEstimate(
            flops=1_000_000_000, bytes_accessed=rows * width, transcendentals=0
        ),
        compiler_params=pltpu.CompilerParams(vmem_limit_bytes=48 * 1024 * 1024),
        name="attend_back",
    )(qkv, grad)


def pack(flat):
    size = flat.shape[-1]
    full = -(-size // 1024) * 1024
    flat = jnp.pad(flat, [(0, 0)] * (flat.ndim - 1) + [(0, full - size)])
    return flat.reshape(flat.shape[:-1] + (full // 128, 128))


def on_device_wide(
    tokens,
    ln1_gain,
    ln1_bias,
    qkv_weight,
    qv_bias,
    out_weight,
    out_bias,
    ln2_gain,
    ln2_bias,
    fc_weight,
    fc_bias,
    proj_weight,
    proj_bias,
    out_grad,
):
    both = ("fsdp", "tensor")
    n_fsdp, n_tensor = lax.axis_size("fsdp"), lax.axis_size("tensor")
    me = lax.axis_index("tensor")
    part = ln1_gain.shape[0]
    width = out_weight.shape[0]
    heads = width // HD
    hidden = fc_weight.shape[1]
    model = tokens.shape[1]
    vectors = jnp.concatenate(
        [
            ln1_gain,
            ln1_bias,
            ln2_gain,
            ln2_bias,
            out_bias,
            proj_bias,
            qv_bias.astype(F32).reshape(-1),
            fc_bias.astype(F32).reshape(-1),
        ]
    )
    bundle = lax.all_gather(pack(vectors), both, axis=0, tiled=False)
    bundle = bundle.reshape(n_fsdp * n_tensor, -1)
    gain_one, bias_one, gain_two, bias_two, bias_out, bias_proj = (
        bundle[:, i * part : (i + 1) * part].reshape(-1) for i in range(6)
    )
    mine = lax.dynamic_index_in_dim(bundle.reshape(n_fsdp, n_tensor, -1), me, 1, keepdims=False)
    low, high = 6 * part, 6 * part + qv_bias.size
    qv_full = (
        mine[:, low:high].reshape((n_fsdp,) + qv_bias.shape).transpose(1, 2, 0, 3).reshape(2, width)
    )
    fcb_full = (
        mine[:, high : high + fc_bias.size]
        .reshape((n_fsdp,) + fc_bias.shape)
        .transpose(1, 0, 2)
        .reshape(hidden)
    )
    bias_row = jnp.concatenate([qv_full[0], jnp.zeros((width,), F32), qv_full[1]])
    joined = lax.all_gather(
        qkv_weight.reshape(qkv_weight.shape[0], 3 * width), "fsdp", axis=0, tiled=True
    )
    out_full = lax.all_gather(out_weight, "fsdp", axis=1, tiled=True)
    fc_full = lax.all_gather(fc_weight, "fsdp", axis=0, tiled=True)
    proj_full = lax.all_gather(proj_weight, "fsdp", axis=1, tiled=True)

    inputs = tokens.astype(F32)
    normed_one = gather_rows(layer_norm(inputs, gain_one, bias_one).astype(BF))
    qkv = in_order([(mm(piece, joined) + bias_row).astype(BF) for piece in normed_one])
    attended = attend(qkv)
    att = [take_rows(attended, k) for k in range(chunk_count())]
    grads = gather_rows(after(out_grad, qkv))
    middle = inputs + (sum_rows(lambda k: mm(att[k], out_full)) + bias_out)
    normed_two = gather_rows(layer_norm(middle, gain_two, bias_two).astype(BF))
    before = [mm(piece, fc_full) + fcb_full for piece in normed_two]
    act = [gelu_tanh(piece).astype(BF) for piece in before]

    grad_pre = []
    for piece, grad in zip(before, grads):
        pull = jax.vjp(gelu_tanh, piece)[1]
        grad_pre.append(pull(mm_t(grad, proj_full))[0].astype(BF))
    grad_normed_two = sum_rows(lambda k: mm_t(grad_pre[k], fc_full))
    grad_pre_all = joined_rows(grad_pre)
    grad_proj = t_mm(joined_rows(act), joined_rows(grads)).astype(BF)
    grad_fc = t_mm(joined_rows(normed_two), grad_pre_all).astype(BF)
    grad_fc_bias = jnp.sum(grad_pre_all, 0, dtype=F32)
    grad_proj_bias = jnp.sum(out_grad, 0, dtype=F32)
    norm_pull_two = jax.vjp(layer_norm, middle, gain_two, bias_two)[1]
    grad_middle_part, grad_gain_two, grad_bias_two = norm_pull_two(grad_normed_two)
    grad_middle = out_grad.astype(F32) + grad_middle_part
    grad_branch = grad_middle.astype(BF)
    grad_out_bias = jnp.sum(grad_branch, 0, dtype=F32)
    branches = gather_rows(grad_branch)
    grad_attended = in_order([mm_t(piece, out_full).astype(BF) for piece in branches])

    late = lax.optimization_barrier((grad_attended, *act))
    grad_attended, act = late[0], late[1:]
    output = middle + sum_rows(lambda k: mm(act[k], proj_full)) + bias_proj
    grad_qkv = attend_back(qkv, grad_attended)
    grad_out = t_mm(joined_rows(att), joined_rows(branches)).astype(BF)
    pieces = [take_rows(grad_qkv, k) for k in range(chunk_count())]
    grad_normed_one = sum_rows(lambda k: mm_t(pieces[k], joined))
    pieces_all = joined_rows(pieces)
    grad_joined = t_mm(joined_rows(normed_one), pieces_all).astype(BF)
    qkv_sums = jnp.sum(pieces_all, 0, dtype=F32)
    norm_pull_one = jax.vjp(layer_norm, inputs, gain_one, bias_one)[1]
    grad_input_part, grad_gain_one, grad_bias_one = norm_pull_one(grad_normed_one)
    input_grad = grad_middle + grad_input_part

    def scatter(value, dim):
        return replica_sum(
            lax.psum_scatter(value, "fsdp", scatter_dimension=dim, tiled=True).astype(BF)
        )

    total_proj = scatter(grad_proj, 1)
    total_fc = scatter(grad_fc, 0)
    total_out = scatter(grad_out, 1)
    total_joined = scatter(grad_joined, 0)

    wide = jnp.stack(
        [grad_gain_one, grad_bias_one, grad_gain_two, grad_bias_two, grad_out_bias, grad_proj_bias]
    )
    wide = wide.reshape(6, n_fsdp * n_tensor, part).transpose(1, 0, 2).reshape(-1, 6 * part)
    grad_qv = jnp.stack([qkv_sums[:width], qkv_sums[2 * width :]])
    grad_qv = grad_qv.reshape(2, heads, n_fsdp, -1).transpose(2, 0, 1, 3).reshape(n_fsdp, -1)
    grad_fcb = grad_fc_bias.reshape(fc_bias.shape[0], n_fsdp, -1).transpose(1, 0, 2)
    own = jnp.concatenate([grad_qv, grad_fcb.reshape(n_fsdp, -1)], -1)
    is_me = (jnp.arange(n_tensor, dtype=jnp.int32) == me)[None, :, None]
    own = jnp.where(is_me, own[:, None, :], 0.0).reshape(n_fsdp * n_tensor, -1)
    sums = lax.psum_scatter(
        pack(jnp.concatenate([wide, own], -1)), both, scatter_dimension=0, tiled=False
    )
    sums = replica_sum(sums).reshape(-1)
    vec = [sums[i * part : (i + 1) * part] for i in range(6)]
    total_qv = sums[low:high].reshape(qv_bias.shape)
    total_fcb = sums[high : high + fc_bias.size].reshape(fc_bias.shape)
    return (
        output,
        input_grad,
        vec[0],
        vec[1],
        total_joined.reshape(qkv_weight.shape),
        total_qv,
        total_out,
        vec[4],
        vec[2],
        vec[3],
        total_fc,
        total_fcb,
        total_proj,
        vec[5],
    )


MESH = pl.DeviceIdType.MESH
HALF = LEN // 2


def chip_swap(value):
    return swap(value, 2)


def y_swap(value):
    return lax.ppermute(value, "replica", [(0, 1), (1, 0)])


def put(full, piece, row, column=0):
    return lax.dynamic_update_slice(full, piece, (row, jnp.int32(column)))


def rows_at(full, row, count):
    return lax.dynamic_slice_in_dim(full, row, count, 0)


def two(first, second, index, dim=0):
    low = jnp.concatenate([first, second], dim)
    high = jnp.concatenate([second, first], dim)
    return jnp.where(index == 0, low, high)


def half_of(value, index, dim):
    low, high = jnp.split(value, 2, dim)
    return jnp.where(index == 0, low, high)


def y_send(value, dim):
    y = lax.axis_index("replica")
    return half_of(value, y, dim), y_swap(half_of(value, 1 - y, dim))


def plus(left, right):
    return (left.astype(F32) + right.astype(F32)).astype(BF)


def group_peer(step):
    n_fsdp, n_tensor = lax.axis_size("fsdp"), lax.axis_size("tensor")
    size = n_fsdp * n_tensor
    me = lax.axis_index("fsdp") * n_tensor + lax.axis_index("tensor")
    peer = lax.rem(me + step, size)
    place = (lax.axis_index("replica"), peer // n_tensor, lax.rem(peer, n_tensor))
    return me, peer, place


def greet(size):
    barrier = pltpu.get_barrier_semaphore()
    for step in range(1, size):
        pl.semaphore_signal(
            barrier, inc=1, device_id=group_peer(step)[2], device_id_type=MESH
        )
    pl.semaphore_wait(barrier, size - 1)


def opening_kernel(
    vec_ref,
    shard_ref,
    fc_ref,
    bundle_ref,
    full_ref,
    fc_all_ref,
    vsend,
    vrecv,
    zsend,
    zrecv,
    xsend,
    xrecv,
    ysend,
    yrecv,
    fsend,
    frecv,
):
    size, count = bundle_ref.shape[0], full_ref.shape[1]
    r, f, t = (lax.axis_index(name) for name in ("replica", "fsdp", "tensor"))
    x_place = (r, f, lax.rem(t + 2, 4))
    y_place = (1 - r, f, t)
    barrier = pltpu.get_barrier_semaphore()
    for step in range(1, size):
        pl.semaphore_signal(
            barrier, inc=1, device_id=group_peer(step)[2], device_id_type=MESH
        )
    pl.semaphore_signal(barrier, inc=1, device_id=y_place, device_id_type=MESH)
    pl.semaphore_wait(barrier, size)

    def send(src, dst, send_sem, recv_sem, place):
        copy = pltpu.make_async_remote_copy(
            src_ref=src,
            dst_ref=dst,
            send_sem=send_sem,
            recv_sem=recv_sem,
            device_id=place,
            device_id_type=MESH,
        )
        copy.start()
        return copy

    along_z = []
    for k in range(1, count):
        place = (r, lax.rem(f + k, count), t)
        along_z.append(
            send(shard_ref.at[r], full_ref.at[0, f, r], zsend.at[k], zrecv.at[k], place)
        )
    rest = []
    for h in range(2):
        rest.append(
            send(shard_ref.at[h], full_ref.at[1, f, h], xsend.at[h], xrecv.at[h], x_place)
        )
    for step in range(1, size):
        me, _, place = group_peer(step)
        rest.append(send(vec_ref, bundle_ref.at[me], vsend.at[step], vrecv.at[step], place))
    for k in range(1, count):
        place = (r, lax.rem(f + k, count), t)
        rest.append(send(fc_ref, fc_all_ref.at[f], fsend.at[k], frecv.at[k], place))
    bundle_ref[group_peer(0)[0]] = vec_ref[...]
    full_ref[0, f] = shard_ref[...]
    fc_all_ref[f] = fc_ref[...]
    along_x = []
    for k in range(1, count):
        along_z[k - 1].wait_recv()
        come = lax.rem(f + count - k, count)
        block = full_ref.at[0, come, r]
        along_x.append(
            send(block, full_ref.at[1, come, r], xsend.at[1 + k], xrecv.at[1 + k], x_place)
        )
        rest.append(send(block, block, ysend.at[k - 1], yrecv.at[k - 1], y_place))
    for k in range(1, count):
        along_x[k - 1].wait_recv()
        come = lax.rem(f + count - k, count)
        block = full_ref.at[1, come, r]
        slot = count + k - 2
        rest.append(send(block, block, ysend.at[slot], yrecv.at[slot], y_place))
    for copy in along_z + along_x:
        copy.wait_send()
    for copy in rest:
        copy.wait()


def small_scatter_kernel(in_ref, out_ref, held, send, recv):
    size = in_ref.shape[0]
    greet(size)
    copies = []
    for step in range(1, size):
        _, peer, place = group_peer(step)
        copy = pltpu.make_async_remote_copy(
            src_ref=in_ref.at[peer],
            dst_ref=held.at[step],
            send_sem=send.at[step],
            recv_sem=recv.at[step],
            device_id=place,
            device_id_type=MESH,
        )
        copy.start()
        copies.append(copy)
    total = in_ref[group_peer(0)[0]]
    for step, copy in enumerate(copies):
        copy.wait()
        total = total + held[step + 1]
    out_ref[...] = total


def opening(vectors, shard, fc_shard, n_fsdp, n_tensor):
    size = n_fsdp * n_tensor
    halves = shard.reshape(2, shard.shape[0] // 2, shard.shape[1])
    whole = pl.BlockSpec(memory_space=pltpu.VMEM)
    dma = pltpu.SemaphoreType.DMA
    return pl.pallas_call(
        opening_kernel,
        in_specs=[whole, whole, whole],
        out_specs=[whole, whole, whole],
        out_shape=[
            jax.ShapeDtypeStruct((size,) + vectors.shape, F32),
            jax.ShapeDtypeStruct((2, n_fsdp) + halves.shape, BF),
            jax.ShapeDtypeStruct((n_fsdp,) + fc_shard.shape, BF),
        ],
        scratch_shapes=[dma((size,)), dma((size,)), dma((n_fsdp,)), dma((n_fsdp,))]
        + [dma((n_fsdp + 1,)), dma((n_fsdp + 1,)), dma((2 * n_fsdp,)), dma((2 * n_fsdp,))]
        + [dma((n_fsdp,)), dma((n_fsdp,))],
        compiler_params=pltpu.CompilerParams(
            collective_id=1, has_side_effects=True, vmem_limit_bytes=32 * 1024 * 1024
        ),
        name="opening",
    )(vectors, halves, fc_shard)


def small_scatter(value):
    size = value.shape[0]
    return pl.pallas_call(
        small_scatter_kernel,
        in_specs=[pl.BlockSpec(memory_space=pltpu.VMEM)],
        out_specs=pl.BlockSpec(memory_space=pltpu.VMEM),
        out_shape=jax.ShapeDtypeStruct(value.shape[1:], F32),
        scratch_shapes=[
            pltpu.VMEM(value.shape, F32),
            pltpu.SemaphoreType.DMA((size,)),
            pltpu.SemaphoreType.DMA((size,)),
        ],
        compiler_params=pltpu.CompilerParams(collective_id=2, has_side_effects=True),
        name="small_scatter",
    )(value)


def attend_own_kernel(qkv_ref, out_ref):
    start = pl.multiple_of((lax.axis_index("tensor") // 2) * HALF, HALF)
    attend_kernel(qkv_ref.at[pl.ds(start, LEN)], out_ref)


def attend_back_own_kernel(qkv_ref, grad_ref, out_ref, keys_sum, values_sum):
    start = pl.multiple_of((lax.axis_index("tensor") // 2) * HALF, HALF)
    rows = pl.ds(start, LEN)
    attend_back_kernel(qkv_ref.at[rows], grad_ref.at[rows], out_ref, keys_sum, values_sum)


def attend_own(qkv):
    rows, width = qkv.shape[0], qkv.shape[1] // 6
    return pl.pallas_call(
        attend_own_kernel,
        grid=(2,),
        in_specs=[pl.BlockSpec((rows, 3 * width), lambda i: (0, i))],
        out_specs=pl.BlockSpec((LEN, width), lambda i: (0, i)),
        out_shape=jax.ShapeDtypeStruct((LEN, 2 * width), BF),
        cost_estimate=pl.CostEstimate(
            flops=1_000_000_000, bytes_accessed=LEN * width, transcendentals=0
        ),
        compiler_params=pltpu.CompilerParams(vmem_limit_bytes=48 * 1024 * 1024),
        name="attend_own",
    )(qkv)


def attend_back_own(qkv, grad, group):
    rows, width = qkv.shape[0], qkv.shape[1] // 6
    return pl.pallas_call(
        attend_back_own_kernel,
        grid=(1,),
        in_specs=[
            pl.BlockSpec((rows, 3 * width), lambda i: (0, group)),
            pl.BlockSpec((rows, width), lambda i: (0, group)),
        ],
        out_specs=pl.BlockSpec((LEN, 3 * width), lambda i: (0, 0)),
        out_shape=jax.ShapeDtypeStruct((LEN, 3 * width), BF),
        scratch_shapes=[pltpu.VMEM((LEN, 2 * HD), F32), pltpu.VMEM((LEN, 2 * HD), F32)],
        cost_estimate=pl.CostEstimate(
            flops=1_000_000_000, bytes_accessed=LEN * width, transcendentals=0
        ),
        compiler_params=pltpu.CompilerParams(vmem_limit_bytes=48 * 1024 * 1024),
        name="attend_back_own",
    )(qkv, grad)


ROOT = (2.0 / 3.141592653589793) ** 0.5


def hidden_kernel(own_ref, side_ref, weight_ref, bias_ref, act_ref, slope_ref):
    rows = own_ref.shape[0]
    for k, ref in enumerate((own_ref, side_ref)):
        for low in range(0, rows, BLOCK):
            pre = mm(ref[low : low + BLOCK], weight_ref[...]) + bias_ref[...]
            square = pre * pre
            bent = jnp.tanh(ROOT * pre * (1.0 + 0.044715 * square))
            half = 0.5 * (1.0 + bent)
            place = slice(k * rows + low, k * rows + low + BLOCK)
            act_ref[place] = (pre * half).astype(BF)
            rise = ROOT * (1.0 + 3 * 0.044715 * square)
            slope = half + 0.5 * pre * (1.0 - bent * bent) * rise
            slope_ref[place] = slope.astype(BF)


def hidden_layer(own, side, weight, bias):
    rows, model = own.shape
    hidden = weight.shape[1]
    size = 256
    whole = pl.BlockSpec((rows, model), lambda i: (0, 0))
    result = pl.BlockSpec((2 * rows, size), lambda i: (0, i))
    return pl.pallas_call(
        hidden_kernel,
        grid=(hidden // size,),
        in_specs=[
            whole,
            whole,
            pl.BlockSpec((model, size), lambda i: (0, i)),
            pl.BlockSpec((1, size), lambda i: (0, i)),
        ],
        out_specs=[result, result],
        out_shape=[jax.ShapeDtypeStruct((2 * rows, hidden), BF)] * 2,
        cost_estimate=pl.CostEstimate(
            flops=1_000_000_000, bytes_accessed=LEN * 256, transcendentals=0
        ),
        compiler_params=pltpu.CompilerParams(vmem_limit_bytes=48 * 1024 * 1024),
        name="hidden_layer",
    )(own, side, weight, bias.reshape(1, hidden))


def hidden_back_kernel(
    grad_ref, proj_ref, slope_ref, weight_ref, pre_ref, sum_ref, own_ref, side_ref, total
):
    step = pl.program_id(0)
    rows = own_ref.shape[0]
    size = proj_ref.shape[0]
    sums = jnp.zeros((1, size), F32)
    for low in range(0, 2 * rows, 3 * BLOCK):
        place = slice(low, low + 3 * BLOCK)
        grad = mm_t(grad_ref[place], proj_ref[...]) * slope_ref[place].astype(F32)
        grad = grad.astype(BF)
        pre_ref[place] = grad
        sums = sums + jnp.sum(grad.astype(F32), 0, keepdims=True)
        part = mm_t(grad, weight_ref[...])

        @pl.when(step == 0)
        def _():
            total[place] = part

        @pl.when(step > 0)
        def _():
            total[place] += part

    sum_ref[...] = sums

    @pl.when(step == pl.num_programs(0) - 1)
    def _():
        own_ref[...] = total[:rows]
        side_ref[...] = total[rows:].astype(BF)


def hidden_back(grads, proj, slope, weight):
    full, model = grads.shape
    hidden = proj.shape[0]
    size = 512
    block = pl.BlockSpec((full, size), lambda i: (0, i))
    half = pl.BlockSpec((full // 2, model), lambda i: (0, 0))
    return pl.pallas_call(
        hidden_back_kernel,
        grid=(hidden // size,),
        in_specs=[
            pl.BlockSpec((full, model), lambda i: (0, 0)),
            pl.BlockSpec((size, model), lambda i: (i, 0)),
            block,
            pl.BlockSpec((model, size), lambda i: (0, i)),
        ],
        out_specs=[block, pl.BlockSpec((1, size), lambda i: (0, i)), half, half],
        out_shape=[
            jax.ShapeDtypeStruct((full, hidden), BF),
            jax.ShapeDtypeStruct((1, hidden), F32),
            jax.ShapeDtypeStruct((full // 2, model), F32),
            jax.ShapeDtypeStruct((full // 2, model), BF),
        ],
        scratch_shapes=[pltpu.VMEM((full, model), F32)],
        cost_estimate=pl.CostEstimate(
            flops=1_000_000_000, bytes_accessed=LEN * 256, transcendentals=0
        ),
        compiler_params=pltpu.CompilerParams(vmem_limit_bytes=52 * 1024 * 1024),
        name="hidden_back",
    )(grads, proj, slope, weight)


def z_scatter(value, dim, earlier):
    count = lax.axis_size("fsdp")
    f = lax.axis_index("fsdp")
    size = value.shape[dim] // count

    def piece(k):
        place = lax.rem(f + k, count) * size
        return lax.dynamic_slice_in_dim(value, place, size, dim)

    total = piece(0).astype(F32)
    for k in range(1, count):
        pairs = [(i, (i + k) % count) for i in range(count)]
        total = total + after(lax.ppermute(piece(k), "fsdp", pairs), earlier).astype(F32)
    return total.astype(BF)


def on_device_chip(
    tokens,
    ln1_gain,
    ln1_bias,
    qkv_weight,
    qv_bias,
    out_weight,
    out_bias,
    ln2_gain,
    ln2_bias,
    fc_weight,
    fc_bias,
    proj_weight,
    proj_bias,
    out_grad,
):
    n_fsdp, n_tensor = lax.axis_size("fsdp"), lax.axis_size("tensor")
    group = n_fsdp * n_tensor
    me = lax.axis_index("tensor")
    x, core = me // 2, me % 2
    y = lax.axis_index("replica")
    part = ln1_gain.shape[0]
    width = out_weight.shape[0]
    heads = width // HD
    hidden = fc_weight.shape[1]
    rows, model = tokens.shape
    mid_row = (1 - x) * LEN
    own_row = x * HALF
    row_of = (core * rows, (1 - core) * rows)

    vectors = jnp.concatenate(
        [
            ln1_gain,
            ln1_bias,
            ln2_gain,
            ln2_bias,
            out_bias,
            proj_bias,
            qv_bias.astype(F32).reshape(-1),
            fc_bias.astype(F32).reshape(-1),
        ]
    )
    flat_qkv = qkv_weight.reshape(qkv_weight.shape[0], 3 * width)
    fc_half = half_of(fc_weight, y, 1)
    bundle, joined, fc_mine = opening(pack(vectors), flat_qkv, fc_half, n_fsdp, n_tensor)
    fc_mine = fc_mine.reshape(model, hidden // 2)
    bundle, joined = bundle.reshape(group, -1), joined.reshape(2, model, 3 * width)
    gain_one, bias_one, gain_two, bias_two, bias_out, bias_proj = (
        bundle[:, i * part : (i + 1) * part].reshape(-1) for i in range(6)
    )
    by_tensor = bundle.reshape(n_fsdp, n_tensor, -1)
    low, high = 6 * part, 6 * part + qv_bias.size
    bias_rows, fcb_rows = [], []
    for place in (me, me ^ 2):
        mine = lax.dynamic_index_in_dim(by_tensor, place, 1, keepdims=False)
        qv = (
            mine[:, low:high]
            .reshape((n_fsdp,) + qv_bias.shape)
            .transpose(1, 2, 0, 3)
            .reshape(2, width)
        )
        bias_rows.append(jnp.concatenate([qv[0], jnp.zeros((width,), F32), qv[1]]))
        fcb = (
            mine[:, high : high + fc_bias.size]
            .reshape((n_fsdp,) + fc_bias.shape)
            .transpose(1, 0, 2)
            .reshape(hidden)
        )
        fcb_rows.append((half_of(fcb, y, 0), half_of(fcb, 1 - y, 0)))
    fcb_full = jnp.concatenate([fcb_rows[j][i] for i in range(2) for j in range(2)])

    proj_and_out = jnp.concatenate([half_of(proj_weight, y, 0), out_weight], 0)
    proj_and_out = lax.all_gather(proj_and_out, "fsdp", axis=1, tiled=True)
    fc_far, fc_back = chip_swap(fc_mine), y_swap(fc_mine)
    def pair(local):
        return [local, swap(local, 1)]

    def pair_sum(term):
        side = swap(term(1).astype(BF), 1)
        return term(0) + side.astype(F32)

    inputs = tokens.astype(F32)
    normed_one = pair(layer_norm(inputs, gain_one, bias_one).astype(BF))
    qkv = jnp.zeros((2 * rows, 6 * width), BF)
    for j in range(2):
        for k in range(2):
            piece = (mm(normed_one[k], joined[j]) + bias_rows[j]).astype(BF)
            qkv = put(qkv, piece, row_of[k], 3 * width * j)
    fc_last = y_swap(after(fc_far, qkv))
    fc_full = jnp.concatenate([fc_mine, fc_far, fc_back, fc_last], 1)
    qkv_mid_half = rows_at(qkv, mid_row, HALF)
    mid_far = chip_swap(after(qkv_mid_half[:, 3 * width :], fc_far))
    att_own = attend_own(after(qkv, fc_far))
    qkv_mid = two(qkv_mid_half[:, : 3 * width], mid_far, x)
    att_mid = attend(after(qkv_mid, fc_last, fc_back))
    proj_and_out = after(proj_and_out, att_own)
    proj_mine, out_near = proj_and_out[: hidden // 2], proj_and_out[hidden // 2 :]
    out_far = chip_swap(out_near)
    out_full = jnp.concatenate([out_near, out_far], 0)
    proj_far, proj_back = chip_swap(proj_mine), y_swap(proj_mine)
    att_far = chip_swap(rows_at(att_mid, (1 - x) * HALF, HALF))
    attended = jnp.zeros((2 * rows, 2 * width), BF)
    attended = put(attended, att_own, own_row)
    attended = put(attended, rows_at(att_mid, x * HALF, HALF), mid_row)
    attended = put(attended, after(att_far, out_far), mid_row, width)
    att = [rows_at(attended, row_of[k], rows) for k in range(2)]
    grads = pair(after(out_grad, qkv))
    middle = inputs + (pair_sum(lambda k: mm(att[k], out_full)) + bias_out)
    normed_two = pair(layer_norm(middle, gain_two, bias_two).astype(BF))
    act_all, slope = hidden_layer(
        normed_two[0], normed_two[1], fc_full, fcb_full
    )
    proj_last = chip_swap(after(proj_back, act_all))
    grads_all = joined_rows(grads)
    proj_sent = t_mm(act_all[:, hidden:], grads_all).astype(BF)
    proj_come = y_swap(proj_sent)
    proj_keep = t_mm(act_all[:, :hidden], after(grads_all, proj_sent)).astype(BF)
    proj_full = after(proj_mine, proj_keep), after(proj_far, proj_keep)
    proj_full += after(proj_back, proj_keep), after(proj_last, proj_keep)
    proj_full = jnp.concatenate(proj_full, 0)
    grad_pre_all, grad_fc_bias, back_here, back_side = hidden_back(
        after(grads_all, proj_keep), proj_full, slope, fc_full
    )
    grad_fc_bias = grad_fc_bias.reshape(-1)
    grad_normed_two = back_here + swap(back_side, 1).astype(F32)
    grad_normed_two = after(grad_normed_two, proj_come)
    grad_proj_bias = jnp.sum(out_grad, 0, dtype=F32)
    norm_pull_two = jax.vjp(layer_norm, middle, gain_two, bias_two)[1]
    grad_middle_part, grad_gain_two, grad_bias_two = norm_pull_two(grad_normed_two)
    grad_middle = out_grad.astype(F32) + grad_middle_part
    grad_branch = grad_middle.astype(BF)
    grad_out_bias = jnp.sum(grad_branch, 0, dtype=F32)
    branches = pair(grad_branch)
    proj_sum = plus(after(proj_keep, grad_branch), proj_come)
    normed_both = joined_rows(normed_two)
    gated_pre = after(grad_pre_all, grad_branch)
    fc_sent = t_mm(normed_both, gated_pre[:, hidden:]).astype(BF)
    fc_come = y_swap(fc_sent)
    fc_keep = t_mm(after(normed_both, fc_sent), gated_pre[:, :hidden]).astype(BF)
    grad_attended = jnp.zeros((2 * rows, 2 * width), BF)
    for k in range(2):
        grad_attended = put(grad_attended, mm_t(branches[k], out_full).astype(BF), row_of[k])

    grad_mid_half = rows_at(grad_attended, mid_row, HALF)
    grad_mid_far = chip_swap(grad_mid_half[:, width:])
    act_late = after(act_all, grad_attended)
    output = pair_sum(lambda k: mm(act_late[k * rows : (k + 1) * rows], proj_full))
    output = middle + output + bias_proj
    grad_mid = two(grad_mid_half[:, :width], grad_mid_far, x)
    back_mid = attend_back(qkv_mid, after(grad_mid, output, fc_keep))
    back_far = chip_swap(rows_at(back_mid, (1 - x) * HALF, HALF))
    half = hidden // 2
    proj_over = chip_swap(after(proj_sum[half:], grad_mid_far))
    proj_part = plus(proj_sum[:half], after(proj_over, back_mid))
    proj_own = lax.psum_scatter(proj_part, "fsdp", scatter_dimension=1, tiled=True).astype(BF)
    cut = 3 * width
    normed_all = joined_rows(normed_one)

    def grads_of(kept, middle_part, own_part):
        full = jnp.zeros((2 * rows, cut), BF)
        full = put(put(full, own_part, own_row), middle_part, mid_row)
        pieces = [rows_at(full, row_of[k], rows) for k in range(2)]
        every = joined_rows(pieces)
        return pieces, jnp.sum(every, 0, dtype=F32), t_mm(normed_all, every).astype(BF)

    own_far = attend_back_own(qkv, after(grad_attended, back_mid, proj_part), 1)
    far_rows, far_totals, joined_far = grads_of(1, after(back_far, own_far), own_far)
    far_keep, far_come = y_send(joined_far, 1)
    own_near = attend_back_own(qkv, after(grad_attended, joined_far, proj_part), 0)
    grad_out = t_mm(joined_rows(att), after(joined_rows(branches), joined_far)).astype(BF)
    out_keep, out_come = y_send(grad_out.reshape(2, width, model), 1)
    fc_sum = plus(fc_keep, after(fc_come, own_far))
    fc_over = chip_swap(after(fc_sum[:, half:], back_far))
    fc_part = plus(fc_sum[:, :half], after(fc_over, own_near))
    near_rows, near_totals, joined_close = grads_of(
        0, rows_at(back_mid, x * HALF, HALF), after(own_near, fc_part, far_come)
    )
    near_keep, near_come = y_send(joined_close, 1)
    far_sum = plus(far_keep, after(far_come, joined_close))
    qkv_over = chip_swap(far_sum)
    qkv_sums = jnp.concatenate([near_totals, far_totals])
    gated = [
        jnp.concatenate([near_rows[k], after(far_rows[k], far_sum)], 1) for k in range(2)
    ]
    joined_both = jnp.concatenate([joined[0], joined[1]], 1)
    out_sum = plus(out_keep, after(out_come, own_near))
    out_over = chip_swap(out_sum[1])
    one_side = mm_t(gated[1], joined_both).astype(BF)
    one_here = mm_t(after(gated[0], one_side), joined_both)
    grad_normed_one = one_here + swap(one_side, 1).astype(F32)
    near_come = after(near_come, one_here)
    near_sum = near_keep.astype(F32) + near_come.astype(F32)
    qkv_part = plus(near_sum, qkv_over)
    fc_own = lax.psum_scatter(fc_part, "fsdp", scatter_dimension=0, tiled=True).astype(BF)
    out_part = plus(out_sum[0], after(out_over, one_side))
    out_own = lax.psum_scatter(out_part, "fsdp", scatter_dimension=1, tiled=True).astype(BF)
    norm_pull_one = jax.vjp(layer_norm, inputs, gain_one, bias_one)[1]
    grad_input_part, grad_gain_one, grad_bias_one = norm_pull_one(grad_normed_one)
    input_grad = grad_middle + grad_input_part
    near_sum = near_keep.astype(F32) + near_come.astype(F32)
    qkv_part = plus(near_sum, qkv_over)

    wide = jnp.stack(
        [grad_gain_one, grad_bias_one, grad_gain_two, grad_bias_two, grad_out_bias, grad_proj_bias]
    )
    wide = wide.reshape(6, group, part).transpose(1, 0, 2).reshape(-1, 6 * part)
    own = []
    for j in range(2):
        sums = qkv_sums[j * cut : (j + 1) * cut]
        grad_qv = jnp.stack([sums[:width], sums[2 * width :]])
        grad_qv = grad_qv.reshape(2, heads, n_fsdp, -1).transpose(2, 0, 1, 3).reshape(n_fsdp, -1)
        first, second = (grad_fc_bias[k * half : (k + 1) * half] for k in (j, 2 + j))
        grad_fcb = two(first, second, y)
        grad_fcb = grad_fcb.reshape(fc_bias.shape[0], n_fsdp, -1).transpose(1, 0, 2)
        own.append(jnp.concatenate([grad_qv, grad_fcb.reshape(n_fsdp, -1)], -1))
    index = jnp.arange(n_tensor, dtype=jnp.int32)[None, :, None]
    own = jnp.where(
        index == me, own[0][:, None, :], jnp.where(index == (me ^ 2), own[1][:, None, :], 0.0)
    ).reshape(group, -1)
    sums = small_scatter(pack(jnp.concatenate([wide, own], -1)))
    qkv_own = z_scatter(qkv_part, 0, sums)
    sums = replica_sum(after(sums, qkv_own)).reshape(-1)
    def whole(mine, dim):
        return two(mine, y_swap(mine), y, dim).astype(F32)

    total_proj = whole(after(proj_own, grad_gain_one), 0)
    total_fc = whole(after(fc_own, sums), 1)
    total_out = whole(after(out_own, sums), 0)
    total_joined = whole(qkv_own, 1)

    vec = [sums[i * part : (i + 1) * part] for i in range(6)]
    total_qv = sums[low:high].reshape(qv_bias.shape)
    total_fcb = sums[high : high + fc_bias.size].reshape(fc_bias.shape)
    return (
        output,
        input_grad,
        vec[0],
        vec[1],
        total_joined.reshape(qkv_weight.shape),
        total_qv,
        total_out,
        vec[4],
        vec[2],
        vec[3],
        total_fc,
        total_fcb,
        total_proj,
        vec[5],
    )


def on_device(*arrays):
    pairs = lax.axis_size("tensor") == 4 and lax.axis_size("replica") == 2
    if pairs and 2 * arrays[0].shape[0] == LEN + HALF:
        return on_device_chip(*arrays)
    return on_device_wide(*arrays)


def solution(mesh):
    placed = (
        P(("replica", "fsdp", "tensor"), None),
        P(("fsdp", "tensor")),
        P(("fsdp", "tensor")),
        P("fsdp", None, "tensor"),
        P(None, "tensor", "fsdp"),
        P("tensor", "fsdp"),
        P(("fsdp", "tensor")),
        P(("fsdp", "tensor")),
        P(("fsdp", "tensor")),
        P("fsdp", "tensor"),
        P("tensor", "fsdp"),
        P("tensor", "fsdp"),
        P(("fsdp", "tensor")),
        P(("replica", "fsdp", "tensor"), None),
    )
    return jax.shard_map(
        on_device,
        mesh=mesh,
        in_specs=placed,
        out_specs=(
            P(("replica", "fsdp", "tensor"), None),
            P(("replica", "fsdp", "tensor"), None),
            P(("fsdp", "tensor")),
            P(("fsdp", "tensor")),
            P("fsdp", None, "tensor"),
            P(None, "tensor", "fsdp"),
            P("tensor", "fsdp"),
            P(("fsdp", "tensor")),
            P(("fsdp", "tensor")),
            P(("fsdp", "tensor")),
            P("fsdp", "tensor"),
            P("tensor", "fsdp"),
            P("tensor", "fsdp"),
            P(("fsdp", "tensor")),
        ),
        check_vma=False,
    )
```

```python
import jax
import jax.numpy as jnp
from jax import lax
from jax.experimental import pallas as pl
from jax.experimental.pallas import tpu as pltpu
from jax.sharding import PartitionSpec as P

HD = 64
LEN = 1024


EPS = 1e-05
NEG = -1e30
BLOCK = 256
BF = jnp.bfloat16
F32 = jnp.float32


def dot(left, right, dims):
    return lax.dot_general(left, right, (dims, ((), ())), preferred_element_type=F32)


def mm(left, right):
    return dot(left, right, ((1,), (0,)))


def mm_t(left, right):
    return dot(left, right, ((1,), (1,)))


def t_mm(left, right):
    return dot(left, right, ((0,), (0,)))


def layer_norm(values, gain, bias):
    center = values - jnp.mean(values, -1, keepdims=True)
    spread = jnp.mean(center * center, -1, keepdims=True)
    return center * lax.rsqrt(spread + EPS) * gain + bias


def gelu_tanh(values):
    return jax.nn.gelu(values, approximate=True)


def swap(value, bit):
    size = lax.axis_size("tensor")
    return lax.ppermute(value, "tensor", [(i, i ^ bit) for i in range(size)])


def after(value, *others):
    return lax.optimization_barrier((value,) + others)[0]


def chunk_count():
    size = lax.axis_size("tensor")
    return 4 if size == 4 else 1


def gather_rows(local):
    if chunk_count() == 1:
        return [lax.all_gather(local, "tensor", axis=0, tiled=True)]
    sib = swap(local, 1)
    far = swap(local, 2)
    return [local, sib, far, swap(far, 1)]


def sum_rows(part):
    if chunk_count() == 1:
        return lax.psum_scatter(part(0), "tensor", scatter_dimension=0, tiled=True)
    side = swap(part(3).astype(BF), 1)
    cross = swap((part(2) + side.astype(F32)).astype(BF), 2)
    near = swap(part(1).astype(BF), 1)
    return part(0) + near.astype(F32) + cross.astype(F32)


def take_rows(full, k):
    if chunk_count() == 1:
        return full
    rows = full.shape[0] // 4
    return lax.dynamic_slice_in_dim(full, (lax.axis_index("tensor") ^ k) * rows, rows, 0)


def in_order(pieces):
    if len(pieces) == 1:
        return pieces[0]
    rows = pieces[0].shape[0]
    me = lax.axis_index("tensor")
    full = jnp.zeros((4 * rows, pieces[0].shape[1]), pieces[0].dtype)
    for k, piece in enumerate(pieces):
        full = lax.dynamic_update_slice_in_dim(full, piece, (me ^ k) * rows, 0)
    return full


def joined_rows(pieces):
    return pieces[0] if len(pieces) == 1 else jnp.concatenate(pieces, 0)


def replica_sum(value):
    size = lax.axis_size("replica")
    if size == 2:
        return value.astype(F32) + lax.ppermute(value, "replica", [(0, 1), (1, 0)]).astype(F32)
    return lax.psum(value, "replica").astype(F32)


def scores_t(qkv_ref, width, head, block):
    stop = (block + 1) * BLOCK
    low = head * HD
    query = qkv_ref[block * BLOCK : stop, low : low + HD]
    keys = qkv_ref[0:stop, width + low : width + low + HD]
    scores = mm_t(keys, query * jnp.asarray(HD ** (-0.5), BF))
    shape = (BLOCK, BLOCK)
    keep = lax.broadcasted_iota(jnp.int32, shape, 0) <= lax.broadcasted_iota(jnp.int32, shape, 1)
    edge = jnp.where(keep, scores[stop - BLOCK :], NEG)
    scores = edge if block == 0 else jnp.concatenate([scores[: stop - BLOCK], edge], 0)
    expo = jnp.exp(scores - jnp.max(scores, 0, keepdims=True))
    return query, keys, expo, 1.0 / jnp.sum(expo, 0, keepdims=True)


def attend_kernel(qkv_ref, out_ref):
    width = out_ref.shape[1]
    for pair in range(width // (2 * HD)):
        for block in range(LEN // BLOCK):
            stop = (block + 1) * BLOCK
            halves = []
            for head in (2 * pair, 2 * pair + 1):
                _, _, expo, inverse = scores_t(qkv_ref, width, head, block)
                low = 2 * width + head * HD
                values = qkv_ref[0:stop, low : low + HD]
                halves.append(t_mm(values, expo.astype(BF)) * inverse)
            out_ref[block * BLOCK : stop, pair * 2 * HD : (pair + 1) * 2 * HD] = (
                jnp.concatenate(halves, 0).T.astype(BF)
            )


def attend_back_kernel(qkv_ref, grad_ref, out_ref, keys_sum, values_sum):
    width = grad_ref.shape[1]
    scale = HD ** (-0.5)
    for pair in range(width // (2 * HD)):
        for block in reversed(range(LEN // BLOCK)):
            stop = (block + 1) * BLOCK
            halves = []
            for side in (0, 1):
                head = 2 * pair + side
                query, keys, expo, inverse = scores_t(qkv_ref, width, head, block)
                low = head * HD
                values = qkv_ref[0:stop, 2 * width + low : 2 * width + low + HD]
                grad = grad_ref[block * BLOCK : stop, low : low + HD]
                probs = expo * inverse
                grad_values = mm(probs.astype(BF), grad)
                grad_probs = mm_t(values, grad)
                weighted = probs * grad_probs
                total = jnp.sum(weighted, 0, keepdims=True)
                grad_scores = (weighted - probs * total).astype(BF)
                grad_keys = mm(grad_scores, query)
                lanes = slice(side * HD, (side + 1) * HD)
                if stop == LEN:
                    values_sum[:, lanes] = grad_values
                    keys_sum[:, lanes] = grad_keys
                else:
                    values_sum[0:stop, lanes] += grad_values
                    keys_sum[0:stop, lanes] += grad_keys
                halves.append(t_mm(keys, grad_scores))
            low = pair * 2 * HD
            out_ref[block * BLOCK : stop, low : low + 2 * HD] = (
                jnp.concatenate(halves, 0).T * scale
            ).astype(BF)
        out_ref[:, width + low : width + low + 2 * HD] = (keys_sum[...] * scale).astype(BF)
        out_ref[:, 2 * width + low : 2 * width + low + 2 * HD] = values_sum[...].astype(BF)


def rows_spec(width):
    return pl.BlockSpec((LEN, width), lambda i: (i, 0))


def attend(qkv):
    rows, width = qkv.shape[0], qkv.shape[1] // 3
    return pl.pallas_call(
        attend_kernel,
        grid=(rows // LEN,),
        in_specs=[rows_spec(3 * width)],
        out_specs=rows_spec(width),
        out_shape=jax.ShapeDtypeStruct((rows, width), BF),
        cost_estimate=pl.CostEstimate(
            flops=1_000_000_000, bytes_accessed=rows * width, transcendentals=0
        ),
        compiler_params=pltpu.CompilerParams(vmem_limit_bytes=48 * 1024 * 1024),
        name="attend",
    )(qkv)


def attend_back(qkv, grad):
    rows, width = grad.shape
    return pl.pallas_call(
        attend_back_kernel,
        grid=(rows // LEN,),
        in_specs=[rows_spec(3 * width), rows_spec(width)],
        out_specs=rows_spec(3 * width),
        out_shape=jax.ShapeDtypeStruct((rows, 3 * width), BF),
        scratch_shapes=[pltpu.VMEM((LEN, 2 * HD), F32), pltpu.VMEM((LEN, 2 * HD), F32)],
        cost_estimate=pl.CostEstimate(
            flops=1_000_000_000, bytes_accessed=rows * width, transcendentals=0
        ),
        compiler_params=pltpu.CompilerParams(vmem_limit_bytes=48 * 1024 * 1024),
        name="attend_back",
    )(qkv, grad)


def pack(flat):
    size = flat.shape[-1]
    full = -(-size // 1024) * 1024
    flat = jnp.pad(flat, [(0, 0)] * (flat.ndim - 1) + [(0, full - size)])
    return flat.reshape(flat.shape[:-1] + (full // 128, 128))


def on_device_wide(
    tokens,
    ln1_gain,
    ln1_bias,
    qkv_weight,
    qv_bias,
    out_weight,
    out_bias,
    ln2_gain,
    ln2_bias,
    fc_weight,
    fc_bias,
    proj_weight,
    proj_bias,
    out_grad,
):
    both = ("fsdp", "tensor")
    n_fsdp, n_tensor = lax.axis_size("fsdp"), lax.axis_size("tensor")
    me = lax.axis_index("tensor")
    part = ln1_gain.shape[0]
    width = out_weight.shape[0]
    heads = width // HD
    hidden = fc_weight.shape[1]
    model = tokens.shape[1]
    vectors = jnp.concatenate(
        [
            ln1_gain,
            ln1_bias,
            ln2_gain,
            ln2_bias,
            out_bias,
            proj_bias,
            qv_bias.astype(F32).reshape(-1),
            fc_bias.astype(F32).reshape(-1),
        ]
    )
    bundle = lax.all_gather(pack(vectors), both, axis=0, tiled=False)
    bundle = bundle.reshape(n_fsdp * n_tensor, -1)
    gain_one, bias_one, gain_two, bias_two, bias_out, bias_proj = (
        bundle[:, i * part : (i + 1) * part].reshape(-1) for i in range(6)
    )
    mine = lax.dynamic_index_in_dim(bundle.reshape(n_fsdp, n_tensor, -1), me, 1, keepdims=False)
    low, high = 6 * part, 6 * part + qv_bias.size
    qv_full = (
        mine[:, low:high].reshape((n_fsdp,) + qv_bias.shape).transpose(1, 2, 0, 3).reshape(2, width)
    )
    fcb_full = (
        mine[:, high : high + fc_bias.size]
        .reshape((n_fsdp,) + fc_bias.shape)
        .transpose(1, 0, 2)
        .reshape(hidden)
    )
    bias_row = jnp.concatenate([qv_full[0], jnp.zeros((width,), F32), qv_full[1]])
    joined = lax.all_gather(
        qkv_weight.reshape(qkv_weight.shape[0], 3 * width), "fsdp", axis=0, tiled=True
    )
    out_full = lax.all_gather(out_weight, "fsdp", axis=1, tiled=True)
    fc_full = lax.all_gather(fc_weight, "fsdp", axis=0, tiled=True)
    proj_full = lax.all_gather(proj_weight, "fsdp", axis=1, tiled=True)

    inputs = tokens.astype(F32)
    normed_one = gather_rows(layer_norm(inputs, gain_one, bias_one).astype(BF))
    qkv = in_order([(mm(piece, joined) + bias_row).astype(BF) for piece in normed_one])
    attended = attend(qkv)
    att = [take_rows(attended, k) for k in range(chunk_count())]
    grads = gather_rows(after(out_grad, qkv))
    middle = inputs + (sum_rows(lambda k: mm(att[k], out_full)) + bias_out)
    normed_two = gather_rows(layer_norm(middle, gain_two, bias_two).astype(BF))
    before = [mm(piece, fc_full) + fcb_full for piece in normed_two]
    act = [gelu_tanh(piece).astype(BF) for piece in before]

    grad_pre = []
    for piece, grad in zip(before, grads):
        pull = jax.vjp(gelu_tanh, piece)[1]
        grad_pre.append(pull(mm_t(grad, proj_full))[0].astype(BF))
    grad_normed_two = sum_rows(lambda k: mm_t(grad_pre[k], fc_full))
    grad_pre_all = joined_rows(grad_pre)
    grad_proj = t_mm(joined_rows(act), joined_rows(grads)).astype(BF)
    grad_fc = t_mm(joined_rows(normed_two), grad_pre_all).astype(BF)
    grad_fc_bias = jnp.sum(grad_pre_all, 0, dtype=F32)
    grad_proj_bias = jnp.sum(out_grad, 0, dtype=F32)
    norm_pull_two = jax.vjp(layer_norm, middle, gain_two, bias_two)[1]
    grad_middle_part, grad_gain_two, grad_bias_two = norm_pull_two(grad_normed_two)
    grad_middle = out_grad.astype(F32) + grad_middle_part
    grad_branch = grad_middle.astype(BF)
    grad_out_bias = jnp.sum(grad_branch, 0, dtype=F32)
    branches = gather_rows(grad_branch)
    grad_attended = in_order([mm_t(piece, out_full).astype(BF) for piece in branches])

    late = lax.optimization_barrier((grad_attended, *act))
    grad_attended, act = late[0], late[1:]
    output = middle + sum_rows(lambda k: mm(act[k], proj_full)) + bias_proj
    grad_qkv = attend_back(qkv, grad_attended)
    grad_out = t_mm(joined_rows(att), joined_rows(branches)).astype(BF)
    pieces = [take_rows(grad_qkv, k) for k in range(chunk_count())]
    grad_normed_one = sum_rows(lambda k: mm_t(pieces[k], joined))
    pieces_all = joined_rows(pieces)
    grad_joined = t_mm(joined_rows(normed_one), pieces_all).astype(BF)
    qkv_sums = jnp.sum(pieces_all, 0, dtype=F32)
    norm_pull_one = jax.vjp(layer_norm, inputs, gain_one, bias_one)[1]
    grad_input_part, grad_gain_one, grad_bias_one = norm_pull_one(grad_normed_one)
    input_grad = grad_middle + grad_input_part

    def scatter(value, dim):
        return replica_sum(
            lax.psum_scatter(value, "fsdp", scatter_dimension=dim, tiled=True).astype(BF)
        )

    total_proj = scatter(grad_proj, 1)
    total_fc = scatter(grad_fc, 0)
    total_out = scatter(grad_out, 1)
    total_joined = scatter(grad_joined, 0)

    wide = jnp.stack(
        [grad_gain_one, grad_bias_one, grad_gain_two, grad_bias_two, grad_out_bias, grad_proj_bias]
    )
    wide = wide.reshape(6, n_fsdp * n_tensor, part).transpose(1, 0, 2).reshape(-1, 6 * part)
    grad_qv = jnp.stack([qkv_sums[:width], qkv_sums[2 * width :]])
    grad_qv = grad_qv.reshape(2, heads, n_fsdp, -1).transpose(2, 0, 1, 3).reshape(n_fsdp, -1)
    grad_fcb = grad_fc_bias.reshape(fc_bias.shape[0], n_fsdp, -1).transpose(1, 0, 2)
    own = jnp.concatenate([grad_qv, grad_fcb.reshape(n_fsdp, -1)], -1)
    is_me = (jnp.arange(n_tensor, dtype=jnp.int32) == me)[None, :, None]
    own = jnp.where(is_me, own[:, None, :], 0.0).reshape(n_fsdp * n_tensor, -1)
    sums = lax.psum_scatter(
        pack(jnp.concatenate([wide, own], -1)), both, scatter_dimension=0, tiled=False
    )
    sums = replica_sum(sums).reshape(-1)
    vec = [sums[i * part : (i + 1) * part] for i in range(6)]
    total_qv = sums[low:high].reshape(qv_bias.shape)
    total_fcb = sums[high : high + fc_bias.size].reshape(fc_bias.shape)
    return (
        output,
        input_grad,
        vec[0],
        vec[1],
        total_joined.reshape(qkv_weight.shape),
        total_qv,
        total_out,
        vec[4],
        vec[2],
        vec[3],
        total_fc,
        total_fcb,
        total_proj,
        vec[5],
    )


MESH = pl.DeviceIdType.MESH
HALF = LEN // 2


def chip_swap(value):
    return swap(value, 2)


def y_swap(value):
    return lax.ppermute(value, "replica", [(0, 1), (1, 0)])


def put(full, piece, row, column=0):
    return lax.dynamic_update_slice(full, piece, (row, jnp.int32(column)))


def rows_at(full, row, count):
    return lax.dynamic_slice_in_dim(full, row, count, 0)


def two(first, second, index, dim=0):
    low = jnp.concatenate([first, second], dim)
    high = jnp.concatenate([second, first], dim)
    return jnp.where(index == 0, low, high)


def half_of(value, index, dim):
    low, high = jnp.split(value, 2, dim)
    return jnp.where(index == 0, low, high)


def y_send(value, dim):
    y = lax.axis_index("replica")
    return half_of(value, y, dim), y_swap(half_of(value, 1 - y, dim))


def plus(left, right):
    return (left.astype(F32) + right.astype(F32)).astype(BF)


def group_peer(step):
    n_fsdp, n_tensor = lax.axis_size("fsdp"), lax.axis_size("tensor")
    size = n_fsdp * n_tensor
    me = lax.axis_index("fsdp") * n_tensor + lax.axis_index("tensor")
    peer = lax.rem(me + step, size)
    place = (lax.axis_index("replica"), peer // n_tensor, lax.rem(peer, n_tensor))
    return me, peer, place


def greet(size):
    barrier = pltpu.get_barrier_semaphore()
    for step in range(1, size):
        pl.semaphore_signal(
            barrier, inc=1, device_id=group_peer(step)[2], device_id_type=MESH
        )
    pl.semaphore_wait(barrier, size - 1)


def opening_kernel(
    vec_ref,
    shard_ref,
    fc_ref,
    bundle_ref,
    full_ref,
    fc_all_ref,
    vsend,
    vrecv,
    zsend,
    zrecv,
    xsend,
    xrecv,
    ysend,
    yrecv,
    fsend,
    frecv,
):
    size, count = bundle_ref.shape[0], full_ref.shape[1]
    r, f, t = (lax.axis_index(name) for name in ("replica", "fsdp", "tensor"))
    x_place = (r, f, lax.rem(t + 2, 4))
    y_place = (1 - r, f, t)
    barrier = pltpu.get_barrier_semaphore()
    for step in range(1, size):
        pl.semaphore_signal(
            barrier, inc=1, device_id=group_peer(step)[2], device_id_type=MESH
        )
    pl.semaphore_signal(barrier, inc=1, device_id=y_place, device_id_type=MESH)
    pl.semaphore_wait(barrier, size)

    def send(src, dst, send_sem, recv_sem, place):
        copy = pltpu.make_async_remote_copy(
            src_ref=src,
            dst_ref=dst,
            send_sem=send_sem,
            recv_sem=recv_sem,
            device_id=place,
            device_id_type=MESH,
        )
        copy.start()
        return copy

    along_z = []
    for k in range(1, count):
        place = (r, lax.rem(f + k, count), t)
        along_z.append(
            send(shard_ref.at[r], full_ref.at[0, f, r], zsend.at[k], zrecv.at[k], place)
        )
    rest = []
    for h in range(2):
        rest.append(
            send(shard_ref.at[h], full_ref.at[1, f, h], xsend.at[h], xrecv.at[h], x_place)
        )
    for step in range(1, size):
        me, _, place = group_peer(step)
        rest.append(send(vec_ref, bundle_ref.at[me], vsend.at[step], vrecv.at[step], place))
    for k in range(1, count):
        place = (r, lax.rem(f + k, count), t)
        rest.append(send(fc_ref, fc_all_ref.at[f], fsend.at[k], frecv.at[k], place))
    bundle_ref[group_peer(0)[0]] = vec_ref[...]
    full_ref[0, f] = shard_ref[...]
    fc_all_ref[f] = fc_ref[...]
    along_x = []
    for k in range(1, count):
        along_z[k - 1].wait_recv()
        come = lax.rem(f + count - k, count)
        block = full_ref.at[0, come, r]
        along_x.append(
            send(block, full_ref.at[1, come, r], xsend.at[1 + k], xrecv.at[1 + k], x_place)
        )
        rest.append(send(block, block, ysend.at[k - 1], yrecv.at[k - 1], y_place))
    for k in range(1, count):
        along_x[k - 1].wait_recv()
        come = lax.rem(f + count - k, count)
        block = full_ref.at[1, come, r]
        slot = count + k - 2
        rest.append(send(block, block, ysend.at[slot], yrecv.at[slot], y_place))
    for copy in along_z + along_x:
        copy.wait_send()
    for copy in rest:
        copy.wait()


def small_scatter_kernel(in_ref, out_ref, held, send, recv):
    size = in_ref.shape[0]
    greet(size)
    copies = []
    for step in range(1, size):
        _, peer, place = group_peer(step)
        copy = pltpu.make_async_remote_copy(
            src_ref=in_ref.at[peer],
            dst_ref=held.at[step],
            send_sem=send.at[step],
            recv_sem=recv.at[step],
            device_id=place,
            device_id_type=MESH,
        )
        copy.start()
        copies.append(copy)
    total = in_ref[group_peer(0)[0]]
    for step, copy in enumerate(copies):
        copy.wait()
        total = total + held[step + 1]
    out_ref[...] = total


def opening(vectors, shard, fc_shard, n_fsdp, n_tensor):
    size = n_fsdp * n_tensor
    halves = shard.reshape(2, shard.shape[0] // 2, shard.shape[1])
    whole = pl.BlockSpec(memory_space=pltpu.VMEM)
    dma = pltpu.SemaphoreType.DMA
    return pl.pallas_call(
        opening_kernel,
        in_specs=[whole, whole, whole],
        out_specs=[whole, whole, whole],
        out_shape=[
            jax.ShapeDtypeStruct((size,) + vectors.shape, F32),
            jax.ShapeDtypeStruct((2, n_fsdp) + halves.shape, BF),
            jax.ShapeDtypeStruct((n_fsdp,) + fc_shard.shape, BF),
        ],
        scratch_shapes=[dma((size,)), dma((size,)), dma((n_fsdp,)), dma((n_fsdp,))]
        + [dma((n_fsdp + 1,)), dma((n_fsdp + 1,)), dma((2 * n_fsdp,)), dma((2 * n_fsdp,))]
        + [dma((n_fsdp,)), dma((n_fsdp,))],
        compiler_params=pltpu.CompilerParams(
            collective_id=1, has_side_effects=True, vmem_limit_bytes=32 * 1024 * 1024
        ),
        name="opening",
    )(vectors, halves, fc_shard)


def small_scatter(value):
    size = value.shape[0]
    return pl.pallas_call(
        small_scatter_kernel,
        in_specs=[pl.BlockSpec(memory_space=pltpu.VMEM)],
        out_specs=pl.BlockSpec(memory_space=pltpu.VMEM),
        out_shape=jax.ShapeDtypeStruct(value.shape[1:], F32),
        scratch_shapes=[
            pltpu.VMEM(value.shape, F32),
            pltpu.SemaphoreType.DMA((size,)),
            pltpu.SemaphoreType.DMA((size,)),
        ],
        compiler_params=pltpu.CompilerParams(collective_id=2, has_side_effects=True),
        name="small_scatter",
    )(value)


def attend_own_kernel(qkv_ref, out_ref):
    start = pl.multiple_of((lax.axis_index("tensor") // 2) * HALF, HALF)
    attend_kernel(qkv_ref.at[pl.ds(start, LEN)], out_ref)


def attend_back_own_kernel(qkv_ref, grad_ref, out_ref, keys_sum, values_sum):
    start = pl.multiple_of((lax.axis_index("tensor") // 2) * HALF, HALF)
    rows = pl.ds(start, LEN)
    attend_back_kernel(qkv_ref.at[rows], grad_ref.at[rows], out_ref, keys_sum, values_sum)


def attend_own(qkv):
    rows, width = qkv.shape[0], qkv.shape[1] // 6
    return pl.pallas_call(
        attend_own_kernel,
        grid=(2,),
        in_specs=[pl.BlockSpec((rows, 3 * width), lambda i: (0, i))],
        out_specs=pl.BlockSpec((LEN, width), lambda i: (0, i)),
        out_shape=jax.ShapeDtypeStruct((LEN, 2 * width), BF),
        cost_estimate=pl.CostEstimate(
            flops=1_000_000_000, bytes_accessed=LEN * width, transcendentals=0
        ),
        compiler_params=pltpu.CompilerParams(vmem_limit_bytes=48 * 1024 * 1024),
        name="attend_own",
    )(qkv)


def attend_back_own(qkv, grad, group):
    rows, width = qkv.shape[0], qkv.shape[1] // 6
    return pl.pallas_call(
        attend_back_own_kernel,
        grid=(1,),
        in_specs=[
            pl.BlockSpec((rows, 3 * width), lambda i: (0, group)),
            pl.BlockSpec((rows, width), lambda i: (0, group)),
        ],
        out_specs=pl.BlockSpec((LEN, 3 * width), lambda i: (0, 0)),
        out_shape=jax.ShapeDtypeStruct((LEN, 3 * width), BF),
        scratch_shapes=[pltpu.VMEM((LEN, 2 * HD), F32), pltpu.VMEM((LEN, 2 * HD), F32)],
        cost_estimate=pl.CostEstimate(
            flops=1_000_000_000, bytes_accessed=LEN * width, transcendentals=0
        ),
        compiler_params=pltpu.CompilerParams(vmem_limit_bytes=48 * 1024 * 1024),
        name="attend_back_own",
    )(qkv, grad)


ROOT = (2.0 / 3.141592653589793) ** 0.5


def hidden_kernel(own_ref, side_ref, weight_ref, bias_ref, act_ref, slope_ref):
    rows = own_ref.shape[0]
    for k, ref in enumerate((own_ref, side_ref)):
        for low in range(0, rows, BLOCK):
            pre = mm(ref[low : low + BLOCK], weight_ref[...]) + bias_ref[...]
            square = pre * pre
            bent = jnp.tanh(ROOT * pre * (1.0 + 0.044715 * square))
            half = 0.5 * (1.0 + bent)
            place = slice(k * rows + low, k * rows + low + BLOCK)
            act_ref[place] = (pre * half).astype(BF)
            rise = ROOT * (1.0 + 3 * 0.044715 * square)
            slope = half + 0.5 * pre * (1.0 - bent * bent) * rise
            slope_ref[place] = slope.astype(BF)


def hidden_layer(own, side, weight, bias):
    rows, model = own.shape
    hidden = weight.shape[1]
    size = 256
    whole = pl.BlockSpec((rows, model), lambda i: (0, 0))
    result = pl.BlockSpec((2 * rows, size), lambda i: (0, i))
    return pl.pallas_call(
        hidden_kernel,
        grid=(hidden // size,),
        in_specs=[
            whole,
            whole,
            pl.BlockSpec((model, size), lambda i: (0, i)),
            pl.BlockSpec((1, size), lambda i: (0, i)),
        ],
        out_specs=[result, result],
        out_shape=[jax.ShapeDtypeStruct((2 * rows, hidden), BF)] * 2,
        cost_estimate=pl.CostEstimate(
            flops=1_000_000_000, bytes_accessed=LEN * 256, transcendentals=0
        ),
        compiler_params=pltpu.CompilerParams(vmem_limit_bytes=48 * 1024 * 1024),
        name="hidden_layer",
    )(own, side, weight, bias.reshape(1, hidden))


def hidden_back_kernel(
    grad_ref, proj_ref, slope_ref, weight_ref, pre_ref, sum_ref, own_ref, side_ref, total
):
    step = pl.program_id(0)
    rows = own_ref.shape[0]
    size = proj_ref.shape[0]
    sums = jnp.zeros((1, size), F32)
    for low in range(0, 2 * rows, 3 * BLOCK):
        place = slice(low, low + 3 * BLOCK)
        grad = mm_t(grad_ref[place], proj_ref[...]) * slope_ref[place].astype(F32)
        grad = grad.astype(BF)
        pre_ref[place] = grad
        sums = sums + jnp.sum(grad.astype(F32), 0, keepdims=True)
        part = mm_t(grad, weight_ref[...])

        @pl.when(step == 0)
        def _():
            total[place] = part

        @pl.when(step > 0)
        def _():
            total[place] += part

    sum_ref[...] = sums

    @pl.when(step == pl.num_programs(0) - 1)
    def _():
        own_ref[...] = total[:rows]
        side_ref[...] = total[rows:].astype(BF)


def hidden_back(grads, proj, slope, weight):
    full, model = grads.shape
    hidden = proj.shape[0]
    size = 512
    block = pl.BlockSpec((full, size), lambda i: (0, i))
    half = pl.BlockSpec((full // 2, model), lambda i: (0, 0))
    return pl.pallas_call(
        hidden_back_kernel,
        grid=(hidden // size,),
        in_specs=[
            pl.BlockSpec((full, model), lambda i: (0, 0)),
            pl.BlockSpec((size, model), lambda i: (i, 0)),
            block,
            pl.BlockSpec((model, size), lambda i: (0, i)),
        ],
        out_specs=[block, pl.BlockSpec((1, size), lambda i: (0, i)), half, half],
        out_shape=[
            jax.ShapeDtypeStruct((full, hidden), BF),
            jax.ShapeDtypeStruct((1, hidden), F32),
            jax.ShapeDtypeStruct((full // 2, model), F32),
            jax.ShapeDtypeStruct((full // 2, model), BF),
        ],
        scratch_shapes=[pltpu.VMEM((full, model), F32)],
        cost_estimate=pl.CostEstimate(
            flops=1_000_000_000, bytes_accessed=LEN * 256, transcendentals=0
        ),
        compiler_params=pltpu.CompilerParams(vmem_limit_bytes=52 * 1024 * 1024),
        name="hidden_back",
    )(grads, proj, slope, weight)


def z_scatter(value, dim, earlier):
    count = lax.axis_size("fsdp")
    f = lax.axis_index("fsdp")
    size = value.shape[dim] // count

    def piece(k):
        place = lax.rem(f + k, count) * size
        return lax.dynamic_slice_in_dim(value, place, size, dim)

    total = piece(0).astype(F32)
    for k in range(1, count):
        pairs = [(i, (i + k) % count) for i in range(count)]
        total = total + after(lax.ppermute(piece(k), "fsdp", pairs), earlier).astype(F32)
    return total.astype(BF)


def on_device_chip(
    tokens,
    ln1_gain,
    ln1_bias,
    qkv_weight,
    qv_bias,
    out_weight,
    out_bias,
    ln2_gain,
    ln2_bias,
    fc_weight,
    fc_bias,
    proj_weight,
    proj_bias,
    out_grad,
):
    n_fsdp, n_tensor = lax.axis_size("fsdp"), lax.axis_size("tensor")
    group = n_fsdp * n_tensor
    me = lax.axis_index("tensor")
    x, core = me // 2, me % 2
    y = lax.axis_index("replica")
    part = ln1_gain.shape[0]
    width = out_weight.shape[0]
    heads = width // HD
    hidden = fc_weight.shape[1]
    rows, model = tokens.shape
    mid_row = (1 - x) * LEN
    own_row = x * HALF
    row_of = (core * rows, (1 - core) * rows)

    vectors = jnp.concatenate(
        [
            ln1_gain,
            ln1_bias,
            ln2_gain,
            ln2_bias,
            out_bias,
            proj_bias,
            qv_bias.astype(F32).reshape(-1),
            fc_bias.astype(F32).reshape(-1),
        ]
    )
    flat_qkv = qkv_weight.reshape(qkv_weight.shape[0], 3 * width)
    fc_half = half_of(fc_weight, y, 1)
    bundle, joined, fc_mine = opening(pack(vectors), flat_qkv, fc_half, n_fsdp, n_tensor)
    fc_mine = fc_mine.reshape(model, hidden // 2)
    bundle, joined = bundle.reshape(group, -1), joined.reshape(2, model, 3 * width)
    gain_one, bias_one, gain_two, bias_two, bias_out, bias_proj = (
        bundle[:, i * part : (i + 1) * part].reshape(-1) for i in range(6)
    )
    by_tensor = bundle.reshape(n_fsdp, n_tensor, -1)
    low, high = 6 * part, 6 * part + qv_bias.size
    bias_rows, fcb_rows = [], []
    for place in (me, me ^ 2):
        mine = lax.dynamic_index_in_dim(by_tensor, place, 1, keepdims=False)
        qv = (
            mine[:, low:high]
            .reshape((n_fsdp,) + qv_bias.shape)
            .transpose(1, 2, 0, 3)
            .reshape(2, width)
        )
        bias_rows.append(jnp.concatenate([qv[0], jnp.zeros((width,), F32), qv[1]]))
        fcb = (
            mine[:, high : high + fc_bias.size]
            .reshape((n_fsdp,) + fc_bias.shape)
            .transpose(1, 0, 2)
            .reshape(hidden)
        )
        fcb_rows.append((half_of(fcb, y, 0), half_of(fcb, 1 - y, 0)))
    fcb_full = jnp.concatenate([fcb_rows[j][i] for i in range(2) for j in range(2)])

    proj_and_out = jnp.concatenate([half_of(proj_weight, y, 0), out_weight], 0)
    proj_and_out = lax.all_gather(proj_and_out, "fsdp", axis=1, tiled=True)
    fc_far, fc_back = chip_swap(fc_mine), y_swap(fc_mine)
    def pair(local):
        return [local, swap(local, 1)]

    def pair_sum(term):
        side = swap(term(1).astype(BF), 1)
        return term(0) + side.astype(F32)

    inputs = tokens.astype(F32)
    normed_one = pair(layer_norm(inputs, gain_one, bias_one).astype(BF))
    qkv = jnp.zeros((2 * rows, 6 * width), BF)
    for j in range(2):
        for k in range(2):
            piece = (mm(normed_one[k], joined[j]) + bias_rows[j]).astype(BF)
            qkv = put(qkv, piece, row_of[k], 3 * width * j)
    fc_last = y_swap(after(fc_far, qkv))
    fc_full = jnp.concatenate([fc_mine, fc_far, fc_back, fc_last], 1)
    qkv_mid_half = rows_at(qkv, mid_row, HALF)
    mid_far = chip_swap(after(qkv_mid_half[:, 3 * width :], fc_far))
    att_own = attend_own(after(qkv, fc_far))
    qkv_mid = two(qkv_mid_half[:, : 3 * width], mid_far, x)
    att_mid = attend(after(qkv_mid, fc_last, fc_back))
    proj_and_out = after(proj_and_out, att_own)
    proj_mine, out_near = proj_and_out[: hidden // 2], proj_and_out[hidden // 2 :]
    out_far = chip_swap(out_near)
    out_full = jnp.concatenate([out_near, out_far], 0)
    proj_far, proj_back = chip_swap(proj_mine), y_swap(proj_mine)
    att_far = chip_swap(rows_at(att_mid, (1 - x) * HALF, HALF))
    attended = jnp.zeros((2 * rows, 2 * width), BF)
    attended = put(attended, att_own, own_row)
    attended = put(attended, rows_at(att_mid, x * HALF, HALF), mid_row)
    attended = put(attended, after(att_far, out_far), mid_row, width)
    att = [rows_at(attended, row_of[k], rows) for k in range(2)]
    grads = pair(after(out_grad, qkv))
    middle = inputs + (pair_sum(lambda k: mm(att[k], out_full)) + bias_out)
    normed_two = pair(layer_norm(middle, gain_two, bias_two).astype(BF))
    act_all, slope = hidden_layer(
        normed_two[0], normed_two[1], fc_full, fcb_full
    )
    proj_last = chip_swap(after(proj_back, act_all))
    grads_all = joined_rows(grads)
    proj_sent = t_mm(act_all[:, hidden:], grads_all).astype(BF)
    proj_come = y_swap(proj_sent)
    proj_keep = t_mm(act_all[:, :hidden], after(grads_all, proj_sent)).astype(BF)
    proj_full = after(proj_mine, proj_keep), after(proj_far, proj_keep)
    proj_full += after(proj_back, proj_keep), after(proj_last, proj_keep)
    proj_full = jnp.concatenate(proj_full, 0)
    grad_pre_all, grad_fc_bias, back_here, back_side = hidden_back(
        after(grads_all, proj_keep), proj_full, slope, fc_full
    )
    grad_fc_bias = grad_fc_bias.reshape(-1)
    grad_normed_two = back_here + swap(back_side, 1).astype(F32)
    grad_normed_two = after(grad_normed_two, proj_come)
    grad_proj_bias = jnp.sum(out_grad, 0, dtype=F32)
    norm_pull_two = jax.vjp(layer_norm, middle, gain_two, bias_two)[1]
    grad_middle_part, grad_gain_two, grad_bias_two = norm_pull_two(grad_normed_two)
    grad_middle = out_grad.astype(F32) + grad_middle_part
    grad_branch = grad_middle.astype(BF)
    grad_out_bias = jnp.sum(grad_branch, 0, dtype=F32)
    branches = pair(grad_branch)
    proj_sum = plus(after(proj_keep, grad_branch), proj_come)
    normed_both = joined_rows(normed_two)
    gated_pre = after(grad_pre_all, grad_branch)
    fc_sent = t_mm(normed_both, gated_pre[:, hidden:]).astype(BF)
    fc_come = y_swap(fc_sent)
    fc_keep = t_mm(after(normed_both, fc_sent), gated_pre[:, :hidden]).astype(BF)
    grad_attended = jnp.zeros((2 * rows, 2 * width), BF)
    for k in range(2):
        grad_attended = put(grad_attended, mm_t(branches[k], out_full).astype(BF), row_of[k])

    grad_mid_half = rows_at(grad_attended, mid_row, HALF)
    grad_mid_far = chip_swap(grad_mid_half[:, width:])
    act_late = after(act_all, grad_attended)
    output = pair_sum(lambda k: mm(act_late[k * rows : (k + 1) * rows], proj_full))
    output = middle + output + bias_proj
    grad_mid = two(grad_mid_half[:, :width], grad_mid_far, x)
    back_mid = attend_back(qkv_mid, after(grad_mid, output, fc_keep))
    back_far = chip_swap(rows_at(back_mid, (1 - x) * HALF, HALF))
    half = hidden // 2
    proj_over = chip_swap(after(proj_sum[half:], grad_mid_far))
    proj_part = plus(proj_sum[:half], after(proj_over, back_mid))
    proj_own = lax.psum_scatter(proj_part, "fsdp", scatter_dimension=1, tiled=True).astype(BF)
    cut = 3 * width
    normed_all = joined_rows(normed_one)

    def grads_of(kept, middle_part, own_part):
        full = jnp.zeros((2 * rows, cut), BF)
        full = put(put(full, own_part, own_row), middle_part, mid_row)
        pieces = [rows_at(full, row_of[k], rows) for k in range(2)]
        every = joined_rows(pieces)
        return pieces, jnp.sum(every, 0, dtype=F32), t_mm(normed_all, every).astype(BF)

    own_far = attend_back_own(qkv, after(grad_attended, back_mid, proj_part), 1)
    far_rows, far_totals, joined_far = grads_of(1, after(back_far, own_far), own_far)
    far_keep, far_come = y_send(joined_far, 1)
    own_near = attend_back_own(qkv, after(grad_attended, joined_far, proj_part), 0)
    grad_out = t_mm(joined_rows(att), after(joined_rows(branches), joined_far)).astype(BF)
    out_keep, out_come = y_send(grad_out.reshape(2, width, model), 1)
    fc_sum = plus(fc_keep, after(fc_come, own_far))
    fc_over = chip_swap(after(fc_sum[:, half:], back_far))
    fc_part = plus(fc_sum[:, :half], after(fc_over, own_near))
    near_rows, near_totals, joined_close = grads_of(
        0, rows_at(back_mid, x * HALF, HALF), after(own_near, fc_part, far_come)
    )
    near_keep, near_come = y_send(joined_close, 1)
    far_sum = plus(far_keep, after(far_come, joined_close))
    qkv_over = chip_swap(far_sum)
    qkv_sums = jnp.concatenate([near_totals, far_totals])
    gated = [
        jnp.concatenate([near_rows[k], after(far_rows[k], far_sum)], 1) for k in range(2)
    ]
    joined_both = jnp.concatenate([joined[0], joined[1]], 1)
    out_sum = plus(out_keep, after(out_come, joined_close))
    out_over = chip_swap(out_sum[1])
    one_side = mm_t(gated[1], joined_both).astype(BF)
    one_here = mm_t(after(gated[0], one_side), joined_both)
    grad_normed_one = one_here + swap(one_side, 1).astype(F32)
    near_come = after(near_come, one_here)
    near_sum = near_keep.astype(F32) + near_come.astype(F32)
    qkv_part = plus(near_sum, qkv_over)
    fc_own = lax.psum_scatter(fc_part, "fsdp", scatter_dimension=0, tiled=True).astype(BF)
    out_part = plus(out_sum[0], after(out_over, grad_normed_one))
    norm_pull_one = jax.vjp(layer_norm, inputs, gain_one, bias_one)[1]
    grad_input_part, grad_gain_one, grad_bias_one = norm_pull_one(grad_normed_one)
    input_grad = grad_middle + grad_input_part
    near_sum = near_keep.astype(F32) + near_come.astype(F32)
    qkv_part = plus(near_sum, qkv_over)

    wide = jnp.stack(
        [grad_gain_one, grad_bias_one, grad_gain_two, grad_bias_two, grad_out_bias, grad_proj_bias]
    )
    wide = wide.reshape(6, group, part).transpose(1, 0, 2).reshape(-1, 6 * part)
    own = []
    for j in range(2):
        sums = qkv_sums[j * cut : (j + 1) * cut]
        grad_qv = jnp.stack([sums[:width], sums[2 * width :]])
        grad_qv = grad_qv.reshape(2, heads, n_fsdp, -1).transpose(2, 0, 1, 3).reshape(n_fsdp, -1)
        first, second = (grad_fc_bias[k * half : (k + 1) * half] for k in (j, 2 + j))
        grad_fcb = two(first, second, y)
        grad_fcb = grad_fcb.reshape(fc_bias.shape[0], n_fsdp, -1).transpose(1, 0, 2)
        own.append(jnp.concatenate([grad_qv, grad_fcb.reshape(n_fsdp, -1)], -1))
    index = jnp.arange(n_tensor, dtype=jnp.int32)[None, :, None]
    own = jnp.where(
        index == me, own[0][:, None, :], jnp.where(index == (me ^ 2), own[1][:, None, :], 0.0)
    ).reshape(group, -1)
    sums = small_scatter(pack(jnp.concatenate([wide, own], -1)))
    qkv_own = z_scatter(qkv_part, 0, sums)
    out_own = z_scatter(out_part, 1, qkv_own)
    sums = replica_sum(after(sums, qkv_own)).reshape(-1)
    def whole(mine, dim):
        return two(mine, y_swap(mine), y, dim).astype(F32)

    total_proj = whole(after(proj_own, sums), 0)
    total_fc = whole(after(fc_own, sums), 1)
    total_out = whole(after(out_own, sums), 0)
    total_joined = whole(qkv_own, 1)

    vec = [sums[i * part : (i + 1) * part] for i in range(6)]
    total_qv = sums[low:high].reshape(qv_bias.shape)
    total_fcb = sums[high : high + fc_bias.size].reshape(fc_bias.shape)
    return (
        output,
        input_grad,
        vec[0],
        vec[1],
        total_joined.reshape(qkv_weight.shape),
        total_qv,
        total_out,
        vec[4],
        vec[2],
        vec[3],
        total_fc,
        total_fcb,
        total_proj,
        vec[5],
    )


def on_device(*arrays):
    pairs = lax.axis_size("tensor") == 4 and lax.axis_size("replica") == 2
    if pairs and 2 * arrays[0].shape[0] == LEN + HALF:
        return on_device_chip(*arrays)
    return on_device_wide(*arrays)


def solution(mesh):
    placed = (
        P(("replica", "fsdp", "tensor"), None),
        P(("fsdp", "tensor")),
        P(("fsdp", "tensor")),
        P("fsdp", None, "tensor"),
        P(None, "tensor", "fsdp"),
        P("tensor", "fsdp"),
        P(("fsdp", "tensor")),
        P(("fsdp", "tensor")),
        P(("fsdp", "tensor")),
        P("fsdp", "tensor"),
        P("tensor", "fsdp"),
        P("tensor", "fsdp"),
        P(("fsdp", "tensor")),
        P(("replica", "fsdp", "tensor"), None),
    )
    return jax.shard_map(
        on_device,
        mesh=mesh,
        in_specs=placed,
        out_specs=(
            P(("replica", "fsdp", "tensor"), None),
            P(("replica", "fsdp", "tensor"), None),
            P(("fsdp", "tensor")),
            P(("fsdp", "tensor")),
            P("fsdp", None, "tensor"),
            P(None, "tensor", "fsdp"),
            P("tensor", "fsdp"),
            P(("fsdp", "tensor")),
            P(("fsdp", "tensor")),
            P(("fsdp", "tensor")),
            P("fsdp", "tensor"),
            P("tensor", "fsdp"),
            P("tensor", "fsdp"),
            P(("fsdp", "tensor")),
        ),
        check_vma=False,
    )
```
